256 devices in a mesh: seq: 32 (over z, x), dp: 8 (over y, core).
Axes of the slice: x: 4, y: 4, z: 8, core: 2. Of those that a mesh axis runs over, the one named last changes fastest.
Arguments:
- tokens: bfloat16 [8, 16384, 4096], P('dp', 'seq'), may hold values from -6 to 6
- w_in: bfloat16 [4096, 2336], P(('seq', 'dp')), may hold values from -0.09375 to 0.09375
- conv_w: float32 [4, 2304], replicated, may hold values from -3 to 3
- a_rate: float32 [32], replicated, may hold values from 3.0517579e-06 to 0.06
- d_skip: float32 [32], replicated, may hold values from 0.5 to 2
- level_w: int32 [8, 11], P('dp'), may hold values from 0 to 256
- lengths: int32 [8], P('dp'), may hold values from 64 to 16384, as said below
Outputs:
- mixed_out: bfloat16 [8, 16384, 2048], P('dp', 'seq')
The draws below stay inside these ranges and needn't reach their ends.
Inputs may be any that keep to these rules, and one draw needn't show every extreme that they name: `lengths`: every length is a multiple of 64, and some request has all 16384 positions live.
All inputs are finite; a program needn't handle non-finite values.
Results may differ from the reference program's by a relative error of at most 0.015.
Values may be sent and summed in bfloat16 or wider, within the bound.
No kernel may reach another device: no remote copies, remote signals or barrier semaphores. Data moves between devices by JAX's collectives and lax.ppermute only.
A program may use at most 128 MiB of HBM per device.

```python
import math
from functools import partial
import jax
import jax.numpy as jnp
import numpy as np
from jax import lax

D = 4096
HEADS = 32
HEAD_DIM = 64
STATE = 128
Q = 64
CONV = 4
LEVELS = 11
CHANNELS = 2304
PROJ = 2336
LENGTH = 16384
REQUESTS = 8


def draw_lengths(key, part):
    stretch_count = jax.random.randint(key, (REQUESTS,), 1, LENGTH // Q + 1)
    chosen = jax.random.randint(jax.random.fold_in(key, 7), (), 0, REQUESTS)
    stretch_count = jnp.where(jnp.arange(REQUESTS) == chosen, LENGTH // Q, stretch_count)
    return (stretch_count * Q).astype(jnp.int32)


def plant(values, own_key, smallest, top_value):
    spot = [jax.random.randint(jax.random.fold_in(own_key, axis), (), 0, length) for axis, length in enumerate(values.shape)]
    main_axis = values.shape.index(max(values.shape))
    neighbour = spot[:main_axis] + [(spot[main_axis] + 1) % values.shape[main_axis]] + spot[main_axis + 1:]
    return values.at[tuple(spot)].set(smallest).at[tuple(neighbour)].set(top_value)


def block_scale(key, extent, shards, least, high):
    def one(axis_at, shards_of):
        steps = jax.random.uniform(jax.random.fold_in(jax.random.fold_in(key, 6), axis_at), (shards_of,), jnp.float32, least / len(shards), high / len(shards))
        return jnp.repeat(jnp.exp(steps), extent[axis_at] // shards_of).reshape((-1,) + (1,) * (len(extent) - axis_at - 1))

    loudness = one(*shards[0])
    for cut in shards[1:]:
        loudness = loudness * one(*cut)
    return loudness


def bell_draw(own_key, extent, deviation, reach, pieces=(), kind=jnp.bfloat16):
    loudness = block_scale(own_key, extent, pieces, -0.22, 0.18) if pieces else 1.0
    drawn = jax.random.normal(own_key, extent, jnp.float32) * deviation * loudness
    return jnp.minimum(jnp.maximum(drawn, -reach), reach).astype(kind)


def setup_inputs(seed: int = 0) -> dict:
    splits = jax.random.split(jax.random.key(seed), 8)
    return {
        "tokens": bell_draw(splits[0], (REQUESTS, LENGTH, D), 1.0, 6.0, ((0, 8), (1, 32))),
        "w_in": bell_draw(splits[1], (D, PROJ), D ** -0.5, 0.09375, ((0, 256),)),
        "conv_w": bell_draw(splits[2], (CONV, CHANNELS), 0.5, 3.0, (), jnp.float32),
        "a_rate": jnp.clip(jnp.exp(jax.random.uniform(splits[3], (HEADS,), jnp.float32, math.log(3.051757857974735e-06), math.log(0.06))), 3.051757857974735e-06, 0.06),
        "d_skip": jnp.clip(jnp.exp(jax.random.uniform(splits[4], (HEADS,), jnp.float32, math.log(0.5), math.log(2.0))), 0.5, 2.0),
        "level_w": plant(jax.random.randint(splits[5], (REQUESTS, LEVELS), 0, 257), jax.random.fold_in(splits[5], 1), 0, 256).astype(jnp.int32),
        "lengths": draw_lengths(jax.random.fold_in(splits[7], 71), 0),
    }


def level_table(count):
    table = np.zeros((count, count), np.int32)
    for later in range(count):
        for earlier in range(later):
            table[later, earlier] = (earlier ^ later).bit_length()
    return table

def one_request(operands, w_in, conv_w, a_rate, d_skip):
    token_rows, level_row, length = operands
    count = token_rows.shape[0]
    channels = conv_w.shape[1]
    inner = channels - 2 * STATE
    projected = jnp.dot(token_rows, w_in, preferred_element_type=jnp.float32)
    raw = projected[:, :channels].astype(jnp.bfloat16)
    padded = jnp.concatenate([jnp.zeros((CONV - 1, channels), jnp.bfloat16), raw], 0)
    convolved = jnp.zeros((count, channels), jnp.float32)
    for offset in range(CONV):
        convolved = convolved + padded[offset:offset + count].astype(jnp.float32) * conv_w[offset]
    values = jax.nn.silu(convolved[:, :inner]).astype(jnp.bfloat16)
    in_b = convolved[:, inner:inner + STATE].astype(jnp.bfloat16)
    out_c = convolved[:, inner + STATE:].astype(jnp.bfloat16)
    step_size = jax.nn.softplus(projected[:, channels:])
    log_decay = -step_size * a_rate[None, :]
    driven = (values.astype(jnp.float32).reshape(count, HEADS, HEAD_DIM) * step_size[:, :, None]).astype(jnp.bfloat16)
    stretches = count // Q
    cumul = jnp.cumsum(log_decay.reshape(stretches, Q, HEADS), axis=1)
    totals = cumul[:, -1]
    before = jnp.cumsum(totals, axis=0) - totals
    level_wt = level_row.astype(jnp.float32) / 256.0
    keys_b = in_b.reshape(stretches, Q, STATE).astype(jnp.float32)
    query_c = out_c.reshape(stretches, Q, STATE).astype(jnp.float32)
    drive_c = driven.reshape(stretches, Q, HEADS, HEAD_DIM).astype(jnp.float32)
    scores = jnp.einsum('ctn,csn->cts', query_c, keys_b)
    causal = jnp.asarray(np.tril(np.ones((Q, Q), bool)))[None, :, :, None]
    differ = cumul[:, :, None, :] - cumul[:, None, :, :]
    inner_wt = jnp.where(causal, jnp.exp(jnp.where(causal, differ, 0.0)), 0.0) * scores[..., None] * level_wt[0]
    inner_wt = inner_wt.astype(jnp.bfloat16)
    y_inner = jnp.einsum('ctsh,cshp->cthp', inner_wt.astype(jnp.float32), drive_c)
    to_end = jnp.exp(totals[:, None, :] - cumul)
    weighted_b = (keys_b[:, :, None, :] * to_end[..., None]).astype(jnp.bfloat16)
    states = jnp.einsum('cshn,cshp->chnp', weighted_b.astype(jnp.float32), drive_c)
    table = jnp.asarray(level_table(stretches))
    lower = jnp.asarray(np.tril(np.ones((stretches, stretches), bool), -1))[:, :, None]
    spacing = before[:, None, :] - before[None, :, :] - totals[None, :, :]
    mixing = jnp.where(lower, jnp.exp(jnp.where(lower, spacing, 0.0)), 0.0) * level_wt[table][:, :, None]
    carried = jnp.einsum('jih,ihnp->jhnp', mixing, states, precision=lax.Precision.HIGHEST)
    carried_low = carried.astype(jnp.bfloat16).astype(jnp.float32)
    y_cross = jnp.exp(cumul)[..., None] * jnp.einsum('ctn,chnp->cthp', query_c, carried_low)
    output = y_inner + y_cross + d_skip[None, None, :, None] * values.astype(jnp.float32).reshape(stretches, Q, HEADS, HEAD_DIM)
    output = output * lax.rsqrt(lax.optimization_barrier(jnp.mean(output * output, axis=-1, keepdims=True)) + 1e-05)
    position = jnp.arange(count, dtype=jnp.int32).reshape(stretches, Q)
    output = jnp.where((position < length)[:, :, None, None], output, 0.0)
    return output.reshape(count, inner).astype(jnp.bfloat16)

def reference(tokens, w_in, conv_w, a_rate, d_skip, level_w, lengths):
    worker = partial(one_request, w_in=w_in, conv_w=conv_w, a_rate=a_rate, d_skip=d_skip)
    return lax.map(worker, (tokens, level_w, lengths))
```

```python
import jax
import jax.numpy as jnp
from jax import lax
from jax.experimental import pallas as pl
from jax.experimental.pallas import tpu as pltpu
from jax.sharding import PartitionSpec as P

STATE = 128
Q = 64
HALO = 16
WIDE = 256
ROWS = 80
F32 = jnp.float32
BF16 = jnp.bfloat16


def dot(a, b):
    return jnp.dot(a, b, preferred_element_type=F32)


def two_parts(x):
    high = x.astype(BF16)
    return high, (x - high.astype(F32)).astype(BF16)


def spread(block, width):
    head = lax.broadcasted_iota(jnp.int32, (2 * 128, width), 0) & 127
    lane = lax.broadcasted_iota(jnp.int32, (2 * 128, width), 1)
    return jnp.where(head == 4 * block + (lane >> 6), 1.0, 0.0).astype(BF16)


def mix_kernel(
    level_ref, tok_ref, w_ref, conv_ref, rate_ref, skip_ref,
    part_ref, send_ref, query_ref, grow_ref,
    proj_s, raw_s, score_s, keys_s, step_s, fade_s, sums_s, sums_t, total_s,
):
    count = part_ref.shape[0]
    step = pl.program_id(0)
    block = step - 2
    proj_s[...] = dot(tok_ref[...], w_ref[...])

    def convolve():
        raw_s[...] = proj_s[...].astype(BF16).astype(F32)
        taps = conv_ref.shape[0]
        total = None
        for tap in range(taps):
            part = raw_s[pl.ds(HALO - taps + 1 + tap, count), :] * conv_ref[tap : tap + 1, :]
            total = part if total is None else total + part
        return total

    @pl.when(step == 0)
    def _():
        mixed = convolve().astype(BF16)
        keys = mixed[:, :STATE]
        query = mixed[:, STATE:]
        query_ref[...] = query
        keys_t = keys.astype(F32).T.astype(BF16)
        keys_s[...] = keys_t
        row = lax.broadcasted_iota(jnp.int32, (count, count), 0)
        col = lax.broadcasted_iota(jnp.int32, (count, count), 1)
        apart = (row >> 6) ^ (col >> 6)
        weight = jnp.where(
            apart == 0,
            level_ref[0],
            jnp.where(apart == 1, level_ref[1], jnp.where(apart < 4, level_ref[2], level_ref[3])),
        )
        score_s[...] = dot(query, keys_t) * jnp.where(col <= row, weight, 0.0)

    @pl.when(step == 1)
    def _():
        x = proj_s[pl.ds(HALO, count), :128]
        lane = lax.broadcasted_iota(jnp.int32, x.shape, 1)
        x = jnp.where(lane < 32, x, 0.0)
        size = jnp.maximum(x, 0.0) + jnp.log1p(jnp.exp(-jnp.abs(x)))
        decay = -size * rate_ref[...]
        row = lax.broadcasted_iota(jnp.int32, (count, count), 0)
        col = lax.broadcasted_iota(jnp.int32, (count, count), 1)
        lower = jnp.where(col <= row, 1.0, 0.0).astype(BF16)
        first = decay.astype(BF16)
        rest = decay - first.astype(F32)
        second = rest.astype(BF16)
        third = (rest - second.astype(F32)).astype(BF16)
        sums = dot(lower, first) + dot(lower, second) + dot(lower, third)
        turned = sums.T
        for group in range(8):
            sums_t[group] = turned[4 * group : 4 * group + 8]
            sums_s[group] = sums if group == 0 else pltpu.roll(sums, 128 - 4 * group, 1)
        high, low = two_parts(size)
        step_s[:, :128] = high
        step_s[:, 128:] = low
        high, low = two_parts(jnp.exp(sums[count - 1 :] - sums))
        fade_s[:, :128] = high
        fade_s[:, 128:] = low
        high, low = two_parts(jnp.exp(sums))
        grow_ref[:, :128] = high
        grow_ref[:, 128:] = low
        total = jnp.broadcast_to(sums[count - 1 :], (16, 128))
        first = total.astype(BF16)
        rest = total - first.astype(F32)
        second = rest.astype(BF16)
        third = (rest - second.astype(F32)).astype(BF16)
        place = lax.broadcasted_iota(jnp.int32, total.shape, 0)
        total_s[...] = jnp.where(
            place == 0,
            first.astype(F32),
            jnp.where(place == 1, second.astype(F32), jnp.where(place == 2, third.astype(F32), 0.0)),
        ).astype(BF16)

    @pl.when(step >= 2)
    def _():
        convolved = convolve()
        values = (convolved * jax.nn.sigmoid(convolved)).astype(BF16).astype(F32)
        lanes = spread(block, WIDE)
        driven = (values * dot(step_s[...], lanes)).astype(BF16)
        faded = (driven.astype(F32) * dot(fade_s[...], lanes)).astype(BF16)
        states = dot(keys_s[...], faded).astype(BF16)
        totals = dot(total_s[...], lanes[:128]).astype(BF16)
        for unit in range(4):
            pair, half = unit // 2, unit % 2
            send_ref[unit, :64] = states[half * 64 : half * 64 + 64, pair * 128 : pair * 128 + 128]
            send_ref[unit, 64:] = totals[:, pair * 128 : pair * 128 + 128]
        side = lax.broadcasted_iota(jnp.int32, (count, 128), 1) < 64
        skipped = values * skip_ref[...]
        for pair in range(2):
            both = driven[:, pair * 128 : pair * 128 + 128]
            sides = (
                jnp.where(side, both, jnp.zeros_like(both)),
                jnp.where(side, jnp.zeros_like(both), both),
            )
            for tile in range(count // 128):
                top, reach = tile * 128, tile * 128 + 128
                total = skipped[top:reach, pair * 128 : pair * 128 + 128]
                score = score_s[top:reach, :reach]
                for half in range(2):
                    head = 2 * pair + half
                    later = sums_s[block, top:reach, head : head + 1]
                    earlier = sums_t[block, head : head + 1, :reach]
                    weight = score * jnp.exp(jnp.minimum(later - earlier, 0.0))
                    total = total + dot(weight.astype(BF16), sides[half][:reach])
                part_ref[top:reach, pair * 128 : pair * 128 + 128] = total


def scan_kernel(level_ref, state_ref, out_ref, sum_s, block_s):
    count = state_ref.shape[0]
    totals = []
    for place in range(count):
        rows = state_ref[place, 64:80].astype(F32)
        totals.append(rows[0:1] + rows[1:2] + rows[2:3])
    before = [jnp.zeros_like(totals[0])]
    for place in range(count - 1):
        before.append(before[-1] + totals[place])
    sum_s[...] = jnp.zeros_like(sum_s)
    for place in range(count):
        block_s[place] = state_ref[place, :64].astype(F32)
    level = 0
    while (1 << level) < count:
        span = 1 << level
        for start in range(span, count, 2 * span):
            previous = block_s[start - span] * level_ref[4 + level]
            for place in range(start, start + span):
                sum_s[place] += jnp.exp(before[place] - before[start]) * previous
            end = start + span
            gone = totals[start]
            for place in range(start + 1, end):
                gone = gone + totals[place]
            block_s[start - span] = block_s[start - span] * jnp.exp(gone) + block_s[start]
        level += 1
    out_ref[...] = sum_s[...].astype(BF16)


def finish_kernel(place_ref, part_ref, state_ref, query_ref, grow_ref, out_ref):
    count = part_ref.shape[0]
    block = pl.program_id(0)
    grow = dot(grow_ref[...], spread(block, WIDE))
    first = lax.broadcasted_iota(jnp.int32, (2 * 128, 128), 0) & 127
    second = lax.broadcasted_iota(jnp.int32, (2 * 128, 128), 1)
    ones = jnp.where((first >> 6) == (second >> 6), 1.0, 0.0).astype(BF16)
    live = place_ref[0] + lax.broadcasted_iota(jnp.int32, (count, 128), 0) < place_ref[1]
    for pair in range(2):
        lanes = slice(pair * 128, pair * 128 + 128)
        state = jnp.concatenate([state_ref[2 * pair], state_ref[2 * pair + 1]], 0)
        y = part_ref[:, lanes] + grow[:, lanes] * dot(query_ref[...], state)
        high, low = two_parts(y * y)
        mean = dot(jnp.concatenate([high, low], 1), ones) * (1.0 / 64.0)
        y = y * lax.rsqrt(mean + 1e-05)
        out_ref[:, lanes] = jnp.where(live, y, 0.0).astype(BF16)


def params():
    return pltpu.CompilerParams(dimension_semantics=("arbitrary",), vmem_limit_bytes=56 * 2**20)


def body(tokens, w_in, conv_w, a_rate, d_skip, level_w, lengths):
    token_rows = tokens.reshape(-1, tokens.shape[-1])
    count, width = token_rows.shape
    taps, channels = conv_w.shape
    heads = a_rate.shape[0]
    inner = channels - 2 * STATE
    head_dim = inner // heads
    blocks = inner // WIDE
    ring = lax.axis_size("seq")
    position = lax.axis_index("seq")
    rim = lax.ppermute(token_rows[count - HALO :], "seq", [(i, i + 1) for i in range(ring - 1)])
    padded = jnp.concatenate([rim, token_rows], 0)
    levels = jnp.concatenate(
        [level_w.reshape(-1).astype(F32) / 256.0, jnp.zeros((16 - level_w.shape[-1],), F32)]
    )
    rate = jnp.concatenate([a_rate, jnp.zeros((128 - heads,), F32)])[None]
    skip = jnp.repeat(d_skip, head_dim)[None]
    weights = lax.all_gather(w_in, ("seq", "dp"), axis=0, tiled=True)
    smem = pl.BlockSpec(memory_space=pltpu.SMEM)

    def column(i):
        return jnp.where(i < 2, blocks + i, i - 2)

    def head_block(i):
        return jnp.maximum(i - 2, 0)

    part, send, query, grow = pl.pallas_call(
        mix_kernel,
        out_shape=(
            jax.ShapeDtypeStruct((count, inner), F32),
            jax.ShapeDtypeStruct((heads, ROWS, 128), BF16),
            jax.ShapeDtypeStruct((count, STATE), BF16),
            jax.ShapeDtypeStruct((count, 256), BF16),
        ),
        grid=(blocks + 2,),
        in_specs=[
            smem,
            pl.BlockSpec((count + HALO, width), lambda i: (0, 0), pipeline_mode=pl.Buffered(1)),
            pl.BlockSpec((width, WIDE), lambda i: (0, column(i))),
            pl.BlockSpec((taps, WIDE), lambda i: (0, jnp.minimum(column(i), blocks))),
            pl.BlockSpec((1, 128), lambda i: (0, 0)),
            pl.BlockSpec((1, WIDE), lambda i: (0, head_block(i))),
        ],
        out_specs=(
            pl.BlockSpec((count, WIDE), lambda i: (0, head_block(i))),
            pl.BlockSpec((4, ROWS, 128), lambda i: (head_block(i), 0, 0)),
            pl.BlockSpec((count, STATE), lambda i: (0, 0)),
            pl.BlockSpec((count, 256), lambda i: (0, 0)),
        ),
        scratch_shapes=[
            pltpu.VMEM((count + HALO, WIDE), F32),
            pltpu.VMEM((count + HALO, WIDE), F32),
            pltpu.VMEM((count, count), F32),
            pltpu.VMEM((STATE, count), BF16),
            pltpu.VMEM((count, 256), BF16),
            pltpu.VMEM((count, 256), BF16),
            pltpu.VMEM((8, count, 128), F32),
            pltpu.VMEM((8, 8, count), F32),
            pltpu.VMEM((16, 128), BF16),
        ],
        compiler_params=params(),
        name="mix",
    )(levels, padded, weights, conv_w, rate, skip)

    gathered = lax.all_to_all(send, "seq", 0, 0, tiled=True)
    scanned = pl.pallas_call(
        scan_kernel,
        out_shape=jax.ShapeDtypeStruct((ring, 64, 128), BF16),
        in_specs=[smem, pl.BlockSpec(memory_space=pltpu.VMEM)],
        out_specs=pl.BlockSpec(memory_space=pltpu.VMEM),
        scratch_shapes=[pltpu.VMEM((ring, 64, 128), F32), pltpu.VMEM((ring, 64, 128), F32)],
        compiler_params=pltpu.CompilerParams(vmem_limit_bytes=32 * 2**20),
        name="scan",
    )(levels, gathered)
    carried = lax.all_to_all(scanned, "seq", 0, 0, tiled=True)

    places = jnp.stack([position * count, lengths[0]]).astype(jnp.int32)
    output = pl.pallas_call(
        finish_kernel,
        out_shape=jax.ShapeDtypeStruct((count, inner), BF16),
        grid=(blocks,),
        in_specs=[
            smem,
            pl.BlockSpec((count, WIDE), lambda i: (0, i)),
            pl.BlockSpec((4, 64, 128), lambda i: (i, 0, 0)),
            pl.BlockSpec((count, STATE), lambda i: (0, 0)),
            pl.BlockSpec((count, 256), lambda i: (0, 0)),
        ],
        out_specs=pl.BlockSpec((count, WIDE), lambda i: (0, i)),
        compiler_params=params(),
        name="finish",
    )(places, part, carried, query, grow)
    return output.reshape(1, count, inner)


def solution(mesh):
    in_specs = (P("dp", "seq", None), P(("seq", "dp"), None), P(), P(), P(), P("dp", None), P("dp"))
    out_specs = P("dp", "seq", None)
    return jax.shard_map(body, mesh=mesh, in_specs=in_specs, out_specs=out_specs, check_vma=False)
```

```python
import jax
import jax.numpy as jnp
from jax import lax
from jax.experimental import pallas as pl
from jax.experimental.pallas import tpu as pltpu
from jax.sharding import PartitionSpec as P


STATE = 128
HALO = 16
WIDE = 256
ROWS = 80
UNIT = 16
SHARE = 11 * UNIT
CHUNKS = 8
SEGMENTS = (
    ((0, 0, 32, 0),),
    ((0, 32, 32, 0),),
    ((0, 64, 32, 0),),
    ((0, 96, 32, 0),),
    ((0, 128, 32, 0),),
    ((0, 160, 16, 0), (1, 0, 16, 16)),
) + tuple(((1, 16 + 32 * i, 32, 0),) for i in range(5))
F32 = jnp.float32
BF16 = jnp.bfloat16


def dot(a, b):
    return jnp.dot(a, b, preferred_element_type=F32)


def two_parts(x):
    high = x.astype(BF16)
    return high, (x - high.astype(F32)).astype(BF16)


def spread(block, width):
    head = lax.broadcasted_iota(jnp.int32, (2 * 128, width), 0) & 127
    lane = lax.broadcasted_iota(jnp.int32, (2 * 128, width), 1)
    return jnp.where(head == 4 * block + (lane >> 6), 1.0, 0.0).astype(BF16)


def split_three(x):
    first = x.astype(BF16)
    rest = x - first.astype(F32)
    second = rest.astype(BF16)
    return first, second, (rest - second.astype(F32)).astype(BF16)


def mix_kernel(
    coord_ref, level_ref, own_ref, other_ref, rims_ref,
    a0, a1, a2, a3, a4, b0, b1, b2, b3, b4,
    conv_ref, rate_ref, skip_ref,
    part_ref, send_ref, query_ref, grow_ref,
    tok_s, w_s, small_s, proj_s, raw_s, score_s, keys_s, step_s, fade_s, sums_s, sums_t, total_s,
    tok_sem, w_sem,
):
    count = own_ref.shape[0]
    pitch = count + HALO
    width = own_ref.shape[1]
    chunk = width // CHUNKS
    step = pl.program_id(0)
    steps = 5
    block = step - 1

    def weight_copies(at):
        slot = at % 2
        columns = (0, 1, 2) if at == 0 else (2 * at + 1, 2 * at + 2)
        copies = []
        for index, column in enumerate(columns):
            if column == 2:
                target, lanes = small_s, slice(0, 128)
            else:
                target, lanes = w_s.at[slot], slice(index * 128, index * 128 + 128)
            for part, row, rows, offset in SEGMENTS[column]:
                into = slice(offset, offset + rows)
                for piece, ref in enumerate(((a0, a1, a2, a3, a4), (b0, b1, b2, b3, b4))[part]):
                    planes = (slice(0, 8), slice(0, 8), slice(0, 8), slice(0, 4), slice(4, 8))[piece]
                    where = coord_ref[4 * part + min(piece, 3)]
                    source = ref.at[:, :, row : row + rows, :]
                    if part == 0:
                        sink = target.at[planes, :, where, into, lanes]
                    else:
                        sink = target.at[planes, where, :, into, lanes]
                    copies.append(pltpu.make_async_copy(source, sink, w_sem.at[slot, len(copies)]))
        return copies

    def token_copies(at):
        lanes = slice(at * chunk, at * chunk + chunk)
        pairs = (
            (rims_ref.at[0:HALO, lanes], tok_s.at[0:HALO, lanes]),
            (own_ref.at[:, lanes], tok_s.at[HALO:pitch, lanes]),
            (rims_ref.at[HALO : 2 * HALO, lanes], tok_s.at[pitch : pitch + HALO, lanes]),
            (other_ref.at[:, lanes], tok_s.at[pitch + HALO : 2 * pitch, lanes]),
        )
        return [
            pltpu.make_async_copy(source, sink, tok_sem.at[at, place])
            for place, (source, sink) in enumerate(pairs)
        ]

    @pl.when(step == 0)
    def _():
        for copy in weight_copies(0):
            copy.start()
        for at in range(CHUNKS):
            for copy in token_copies(at):
                copy.start()
        for copy in weight_copies(1):
            copy.start()
        for copy in weight_copies(0):
            copy.wait()

    for at in range(1, steps):

        @pl.when(step == at)
        def _(at=at):
            if at + 1 < steps:
                for copy in weight_copies(at + 1):
                    copy.start()
            for copy in weight_copies(at):
                copy.wait()

    def convolve(request):
        taps = conv_ref.shape[0]
        total = None
        for tap in range(taps):
            start = request * pitch + HALO - taps + 1 + tap
            part = raw_s[pl.ds(start, count), :] * conv_ref[tap : tap + 1, :]
            total = part if total is None else total + part
        return total

    @pl.when(step == 0)
    def _():
        planes = 8 // CHUNKS
        both = None
        for at in range(CHUNKS):
            for copy in token_copies(at):
                copy.wait()
            token = tok_s[:, at * chunk : at * chunk + chunk]
            main = dot(token, w_s[0, at * planes : (at + 1) * planes].reshape(chunk, WIDE))
            small = dot(token, small_s[at * planes : (at + 1) * planes].reshape(chunk, 128))
            if at == 0:
                proj_s[...] = main
                raw_s[:, :128] = small
            else:
                proj_s[...] += main
                raw_s[:, :128] += small
        row = lax.broadcasted_iota(jnp.int32, (count, count), 0)
        col = lax.broadcasted_iota(jnp.int32, (count, count), 1)
        lower = jnp.where(col <= row, 1.0, 0.0).astype(BF16)
        for request in range(2):
            x = raw_s[pl.ds(request * pitch + HALO, count), :128]
            size = jnp.maximum(x, 0.0) + jnp.log1p(jnp.exp(-jnp.abs(x)))
            first, second, third = split_three(-size * rate_ref[...])
            sums = dot(lower, first) + dot(lower, second) + dot(lower, third)
            turned = sums.T
            for group in range(4):
                sums_t[request, group] = turned[4 * group : 4 * group + 8]
                sums_s[request, group] = sums if group == 0 else pltpu.roll(sums, 128 - 4 * group, 1)
            step_s[request, :, :128], step_s[request, :, 128:] = two_parts(size)
            fade = jnp.exp(sums[count - 1 :] - sums)
            fade_s[request, :, :128], fade_s[request, :, 128:] = two_parts(fade)
            grow_ref[request, :, :128], grow_ref[request, :, 128:] = two_parts(jnp.exp(sums))
            first, second, third = split_three(jnp.broadcast_to(sums[count - 1 :], (16, 128)))
            place = lax.broadcasted_iota(jnp.int32, (16, 128), 0)
            total = jnp.where(
                place == 0,
                first.astype(F32),
                jnp.where(
                    place == 1, second.astype(F32), jnp.where(place == 2, third.astype(F32), 0.0)
                ),
            )
            total_s[request] = total.astype(BF16)
        raw_s[...] = proj_s[...].astype(BF16).astype(F32)
        apart = (row >> 6) ^ (col >> 6)
        for request in range(2):
            mixed = convolve(request).astype(BF16)
            query = mixed[:, STATE:]
            query_ref[request] = query
            keys_t = mixed[:, :STATE].astype(F32).T.astype(BF16)
            keys_s[request] = keys_t
            weight = jnp.where(
                apart == 0,
                level_ref[request, 0],
                jnp.where(
                    apart == 1,
                    level_ref[request, 1],
                    jnp.where(apart < 4, level_ref[request, 2], level_ref[request, 3]),
                ),
            )
            score_s[request] = dot(query, keys_t) * jnp.where(col <= row, weight, 0.0)

    @pl.when(step >= 1)
    def _():
        raw_s[...] = dot(tok_s[...], w_s[step % 2].reshape(width, WIDE)).astype(BF16).astype(F32)
        lanes = spread(block, WIDE)
        side = lax.broadcasted_iota(jnp.int32, (count, 128), 1) < 64
        for request in range(2):
            convolved = convolve(request)
            values = (convolved * jax.nn.sigmoid(convolved)).astype(BF16).astype(F32)
            driven = (values * dot(step_s[request], lanes)).astype(BF16)
            faded = (driven.astype(F32) * dot(fade_s[request], lanes)).astype(BF16)
            states = dot(keys_s[request], faded).astype(BF16)
            totals = dot(total_s[request], lanes[:128]).astype(BF16)
            for unit in range(4):
                pair, half = unit // 2, unit % 2
                cut = slice(pair * 128, pair * 128 + 128)
                send_ref[request, unit, :64] = states[half * 64 : half * 64 + 64, cut]
                send_ref[request, unit, 64:] = totals[:, cut]
            skipped = values * skip_ref[...]
            for pair in range(2):
                cut = slice(pair * 128, pair * 128 + 128)
                both = driven[:, cut]
                sides = (
                    jnp.where(side, both, jnp.zeros_like(both)),
                    jnp.where(side, jnp.zeros_like(both), both),
                )
                for tile in range(count // 128):
                    top, reach = tile * 128, tile * 128 + 128
                    total = skipped[top:reach, cut]
                    score = score_s[request, top:reach, :reach]
                    for half in range(2):
                        head = 2 * pair + half
                        later = sums_s[request, block, top:reach, head : head + 1]
                        earlier = sums_t[request, block, head : head + 1, :reach]
                        weight = score * jnp.exp(jnp.minimum(later - earlier, 0.0))
                        total = total + dot(weight.astype(BF16), sides[half][:reach])
                    part_ref[request, top:reach, cut] = total


def order_z_kernel(coord_ref, *refs):
    pieces, (first_ref, second_ref, sem) = refs[:9], refs[9:]
    copies = []
    for place in range(7):
        where = coord_ref[8 + place]
        copies.append((pieces[place].at[0], first_ref.at[where]))
        copies.append((pieces[place].at[1], second_ref.at[where]))
    copies.append((pieces[7].at[0], first_ref.at[coord_ref[15]]))
    copies.append((pieces[8].at[0], second_ref.at[coord_ref[15]]))
    run_copies(copies, sem)


def order_kernel(base, coord_ref, *refs):
    pieces, (out_ref, sem) = refs[:5], refs[5:]
    copies = []
    for place in range(5):
        planes = (slice(0, 8), slice(0, 8), slice(0, 8), slice(0, 4), slice(4, 8))[place]
        copies.append((pieces[place], out_ref.at[planes, coord_ref[base + min(place, 3)]]))
    run_copies(copies, sem)


def run_copies(pairs, sem):
    copies = [pltpu.make_async_copy(a, b, sem.at[i]) for i, (a, b) in enumerate(pairs)]
    for copy in copies:
        copy.start()
    for copy in copies:
        copy.wait()


def scan_kernel(level_ref, state_ref, out_ref, sum_s, block_s):
    count = state_ref.shape[0]
    totals = []
    for place in range(count):
        rows = state_ref[place, 64:80].astype(F32)
        totals.append(rows[0:1] + rows[1:2] + rows[2:3])
    before = [jnp.zeros_like(totals[0])]
    for place in range(count - 1):
        before.append(before[-1] + totals[place])
    sum_s[...] = jnp.zeros_like(sum_s)
    for place in range(count):
        block_s[place] = state_ref[place, :64].astype(F32)
    level = 0
    while (1 << level) < count:
        span = 1 << level
        for start in range(span, count, 2 * span):
            previous = block_s[start - span] * level_ref[4 + level]
            for place in range(start, start + span):
                sum_s[place] += jnp.exp(before[place] - before[start]) * previous
            end = start + span
            gone = totals[start]
            for place in range(start + 1, end):
                gone = gone + totals[place]
            block_s[start - span] = block_s[start - span] * jnp.exp(gone) + block_s[start]
        level += 1
    out_ref[...] = sum_s[...].astype(BF16)


def finish_kernel(place_ref, part_ref, state_ref, query_ref, grow_ref, out_ref):
    count = part_ref.shape[1]
    block = pl.program_id(0)
    grow = dot(grow_ref[0], spread(block, WIDE))
    first = lax.broadcasted_iota(jnp.int32, (2 * 128, 128), 0) & 127
    second = lax.broadcasted_iota(jnp.int32, (2 * 128, 128), 1)
    ones = jnp.where((first >> 6) == (second >> 6), 1.0, 0.0).astype(BF16)
    live = place_ref[1] + lax.broadcasted_iota(jnp.int32, (count, 128), 0) < place_ref[2]
    for pair in range(2):
        lanes = slice(pair * 128, pair * 128 + 128)
        state = jnp.concatenate([state_ref[2 * pair], state_ref[2 * pair + 1]], 0)
        y = part_ref[0, :, lanes] + grow[:, lanes] * dot(query_ref[0], state)
        high, low = two_parts(y * y)
        mean = dot(jnp.concatenate([high, low], 1), ones) * (1.0 / 64.0)
        y = y * lax.rsqrt(mean + 1e-05)
        out_ref[:, lanes] = jnp.where(live, y, 0.0).astype(BF16)


def params():
    return pltpu.CompilerParams(dimension_semantics=("arbitrary",), vmem_limit_bytes=56 * 2**20)


ANY = pl.BlockSpec(memory_space=pl.ANY)
SMEM = pl.BlockSpec(memory_space=pltpu.SMEM)


def near(i):
    return i ^ 1


def far(i):
    return ((i + 1) ^ 1) - 1


def along_z(value, move):
    return lax.ppermute(value, "seq", [(i, move(i // 4) % 8 * 4 + i % 4) for i in range(32)])


def along_x(value, move):
    return lax.ppermute(value, "seq", [(i, i // 4 * 4 + move(i % 4) % 4) for i in range(32)])


def along_y(value, move):
    return lax.ppermute(value, "dp", [(i, move(i // 2) % 4 * 2 + i % 2) for i in range(8)])


def to_twin(value):
    return lax.ppermute(value, "dp", [(i, i ^ 1) for i in range(8)])


def ring_of_four(value, along):
    half = value.shape[0] // 2
    first = along(value, near)
    second = along(value, far)
    return (value, first, second, along(second[:half], near), along(first[half:], far))


def ordered(pieces, coords, base, name):
    shape = pieces[0].shape
    return pl.pallas_call(
        lambda *refs: order_kernel(base, *refs),
        out_shape=jax.ShapeDtypeStruct((shape[0], 4) + shape[1:], BF16),
        in_specs=[SMEM] + [ANY] * 5,
        out_specs=ANY,
        scratch_shapes=[pltpu.SemaphoreType.DMA((5,))],
        name=name,
    )(coords, *pieces)


def gather_weights(w_in, core, coords):
    depth = w_in.shape[0]
    tiles = w_in[:, :2304].reshape(depth, 18, 128).transpose(1, 0, 2)

    def share(of):
        small = lax.dynamic_slice(w_in, (0, 2304 + 16 * of), (depth, 16))
        small = jnp.pad(small, ((0, 0), (0, 112)))[None]
        return jnp.concatenate([tiles[16:], small, lax.dynamic_slice_in_dim(tiles, 8 * of, 8)], 0)

    mine = share(core)
    got = to_twin(share(1 - core))
    low = jnp.where(core == 0, mine, got)
    high = jnp.where(core == 0, got, mine)
    start = jnp.stack([low, high], 1).reshape(2, SHARE, 128)
    a1, b1 = along_z(start, near), along_z(start, far)
    a2, b2 = along_z(b1, near), along_z(a1, far)
    a3, b3 = along_z(b2, near), along_z(a2, far)
    a4, b4 = along_z(b3[:1], near), along_z(a3[1:], far)
    first, second = pl.pallas_call(
        order_z_kernel,
        out_shape=(jax.ShapeDtypeStruct((8, SHARE, 128), BF16),) * 2,
        in_specs=[SMEM] + [ANY] * 9,
        out_specs=(ANY, ANY),
        scratch_shapes=[pltpu.SemaphoreType.DMA((16,))],
        name="order_z",
    )(coords, start, a1, b1, a2, b2, a3, b3, a4, b4)
    first = ordered(ring_of_four(first, along_x), coords, 4, "order_x")
    second = ordered(ring_of_four(second, along_y), coords, 0, "order_y")
    return ring_of_four(first, along_y) + ring_of_four(second, along_x)


def body(tokens, w_in, conv_w, a_rate, d_skip, level_w, lengths):
    token_rows = tokens.reshape(-1, tokens.shape[-1])
    count, width = token_rows.shape
    taps, channels = conv_w.shape
    heads = a_rate.shape[0] // 2
    inner = (channels - 2 * STATE) // 2
    head_dim = inner // heads
    blocks = inner // WIDE
    ring = lax.axis_size("seq")
    position = lax.axis_index("seq")
    line = lax.axis_index("dp")
    core = line % 2
    y, x, z = line // 2, position % 4, position // 4

    def hop(i):
        return jnp.mod(((i + 1) ^ 1) - 1, 8)

    trail = [z, z ^ 1, hop(z)]
    trail += [hop(z ^ 1), hop(z) ^ 1]
    trail += [trail[4 - 1] ^ 1, hop(trail[4])]
    trail += [jnp.mod(z + 4, 8)]
    coords = jnp.stack([y, y ^ 1, 3 - y, y ^ 2, x, x ^ 1, 3 - x, x ^ 2] + trail).astype(jnp.int32)

    pieces = gather_weights(w_in, core, coords)
    other_rows = to_twin(token_rows)
    tails = jnp.concatenate([token_rows[count - HALO :], other_rows[count - HALO :]], 0)
    rims = lax.ppermute(tails, "seq", [(i, i + 1) for i in range(ring - 1)])
    facts = jnp.concatenate([level_w.reshape(-1), lengths, jnp.zeros((4,), jnp.int32)])
    facts = jnp.stack([facts, to_twin(facts)])
    levels = facts.astype(F32) / 256.0

    rate = jnp.pad(lax.dynamic_slice(a_rate, (core * heads,), (heads,)), (0, 128 - heads))[None]
    skip = jnp.repeat(lax.dynamic_slice(d_skip, (core * heads,), (heads,)), head_dim)[None]
    conv = jnp.concatenate(
        [conv_w[:, 2 * inner :], lax.dynamic_slice(conv_w, (0, core * inner), (taps, inner))], 1
    )

    def head_block(i):
        return jnp.maximum(i - 1, 0)

    part, send, query, grow = pl.pallas_call(
        mix_kernel,
        out_shape=(
            jax.ShapeDtypeStruct((2, count, inner), F32),
            jax.ShapeDtypeStruct((2, heads, ROWS, 128), BF16),
            jax.ShapeDtypeStruct((2, count, STATE), BF16),
            jax.ShapeDtypeStruct((2, count, 256), BF16),
        ),
        grid=(blocks + 1,),
        in_specs=[SMEM, SMEM]
        + [ANY] * 13
        + [
            pl.BlockSpec((taps, WIDE), lambda i: (0, i)),
            pl.BlockSpec((1, 128), lambda i: (0, 0)),
            pl.BlockSpec((1, WIDE), lambda i: (0, head_block(i))),
        ],
        out_specs=(
            pl.BlockSpec((2, count, WIDE), lambda i: (0, 0, head_block(i))),
            pl.BlockSpec((2, 4, ROWS, 128), lambda i: (0, head_block(i), 0, 0)),
            pl.BlockSpec((2, count, STATE), lambda i: (0, 0, 0)),
            pl.BlockSpec((2, count, 256), lambda i: (0, 0, 0)),
        ),
        scratch_shapes=[
            pltpu.VMEM((2 * (count + HALO), width), BF16),
            pltpu.VMEM((2, 8, 4, 4, 32, WIDE), BF16),
            pltpu.VMEM((8, 4, 4, 32, 128), BF16),
            pltpu.VMEM((2 * (count + HALO), WIDE), F32),
            pltpu.VMEM((2 * (count + HALO), WIDE), F32),
            pltpu.VMEM((2, count, count), F32),
            pltpu.VMEM((2, STATE, count), BF16),
            pltpu.VMEM((2, count, 256), BF16),
            pltpu.VMEM((2, count, 256), BF16),
            pltpu.VMEM((2, 4, count, 128), F32),
            pltpu.VMEM((2, 4, 8, count), F32),
            pltpu.VMEM((2, 16, 128), BF16),
            pltpu.SemaphoreType.DMA((CHUNKS, 4)),
            pltpu.SemaphoreType.DMA((2, 15)),
        ],
        compiler_params=params(),
        name="mix",
    )(coords, levels, token_rows, other_rows, rims, *pieces, conv, rate, skip)

    gathered = lax.all_to_all(send.reshape(ring, ROWS, 128), "seq", 0, 0, tiled=True)
    scanned = pl.pallas_call(
        scan_kernel,
        out_shape=jax.ShapeDtypeStruct((ring, 64, 128), BF16),
        in_specs=[SMEM, pl.BlockSpec(memory_space=pltpu.VMEM)],
        out_specs=pl.BlockSpec(memory_space=pltpu.VMEM),
        scratch_shapes=[pltpu.VMEM((ring, 64, 128), F32), pltpu.VMEM((ring, 64, 128), F32)],
        compiler_params=pltpu.CompilerParams(vmem_limit_bytes=32 * 2**20),
        name="scan",
    )(jnp.where(position < 16, levels[0], levels[1]), gathered)
    carried = lax.all_to_all(scanned, "seq", 0, 0, tiled=True)

    def finish(request, columns, column):
        places = jnp.stack([column, position * count, facts[request, 11]]).astype(jnp.int32)
        return pl.pallas_call(
            finish_kernel,
            out_shape=jax.ShapeDtypeStruct((count, columns), BF16),
            grid_spec=pltpu.PrefetchScalarGridSpec(
                num_scalar_prefetch=1,
                grid=(blocks,),
                in_specs=[
                    pl.BlockSpec((1, count, WIDE), lambda i, at: (request, 0, i)),
                    pl.BlockSpec((4, 64, 128), lambda i, at: (4 * request + i, 0, 0)),
                    pl.BlockSpec((1, count, STATE), lambda i, at: (request, 0, 0)),
                    pl.BlockSpec((1, count, 256), lambda i, at: (request, 0, 0)),
                ],
                out_specs=pl.BlockSpec((count, WIDE), lambda i, at: (0, at[0] + i)),
            ),
            compiler_params=params(),
            name="finish",
        )(places, part, carried, query, grow)

    returned = to_twin(finish(1, inner, jnp.int32(0)))
    output = finish(0, 2 * inner, core * blocks)
    output = lax.dynamic_update_slice(output, returned, (0, (1 - core) * inner))
    return output.reshape(1, count, 2 * inner)


def solution(mesh):
    in_specs = (P("dp", "seq", None), P(("seq", "dp"), None), P(), P(), P(), P("dp", None), P("dp"))
    out_specs = P("dp", "seq", None)
    return jax.shard_map(body, mesh=mesh, in_specs=in_specs, out_specs=out_specs, check_vma=False)
```

```python
import jax
import jax.numpy as jnp
from jax import lax
from jax.experimental import pallas as pl
from jax.experimental.pallas import tpu as pltpu
from jax.sharding import PartitionSpec as P


STATE = 128
HALO = 16
WIDE = 256
ROWS = 80
UNIT = 16
SHARE = 11 * UNIT
CHUNKS = 8
SEGMENTS = (
    ((0, 0, 32, 0),),
    ((0, 32, 32, 0),),
    ((0, 64, 32, 0),),
    ((0, 96, 32, 0),),
    ((0, 128, 32, 0),),
    ((0, 160, 16, 0), (1, 0, 16, 16)),
) + tuple(((1, 16 + 32 * i, 32, 0),) for i in range(5))
F32 = jnp.float32
BF16 = jnp.bfloat16


def dot(a, b):
    return jnp.dot(a, b, preferred_element_type=F32)


def two_parts(x):
    high = x.astype(BF16)
    return high, (x - high.astype(F32)).astype(BF16)


def spread(block, width):
    head = lax.broadcasted_iota(jnp.int32, (2 * 128, width), 0) & 127
    lane = lax.broadcasted_iota(jnp.int32, (2 * 128, width), 1)
    return jnp.where(head == 4 * block + (lane >> 6), 1.0, 0.0).astype(BF16)


def split_three(x):
    first = x.astype(BF16)
    rest = x - first.astype(F32)
    second = rest.astype(BF16)
    return first, second, (rest - second.astype(F32)).astype(BF16)


def mix_kernel(
    coord_ref, level_ref, own_ref, other_ref, rims_ref,
    a0, a1, a2, a3, a4, b0, b1, b2, b3, b4,
    conv_ref, rate_ref,
    values_ref, driven_ref, send_ref, query_ref, grow_ref, score_s, sums_s, sums_t,
    tok_s, w_s, small_s, proj_s, raw_s, keys_s, step_s, fade_s, total_s,
    tok_sem, w_sem,
):
    count = own_ref.shape[0]
    pitch = count + HALO
    width = own_ref.shape[1]
    chunk = width // CHUNKS
    step = pl.program_id(0)
    steps = 5
    block = step - 1

    def weight_copies(at):
        slot = at % 2
        columns = (0, 1, 2) if at == 0 else (2 * at + 1, 2 * at + 2)
        copies = []
        for index, column in enumerate(columns):
            if column == 2:
                target, lanes = small_s, slice(0, 128)
            else:
                target, lanes = w_s.at[slot], slice(index * 128, index * 128 + 128)
            for part, row, rows, offset in SEGMENTS[column]:
                into = slice(offset, offset + rows)
                for piece, ref in enumerate(((a0, a1, a2, a3, a4), (b0, b1, b2, b3, b4))[part]):
                    planes = (slice(0, 8), slice(0, 8), slice(0, 8), slice(0, 4), slice(4, 8))[piece]
                    where = coord_ref[4 * part + min(piece, 3)]
                    source = ref.at[:, :, row : row + rows, :]
                    if part == 0:
                        sink = target.at[planes, :, where, into, lanes]
                    else:
                        sink = target.at[planes, where, :, into, lanes]
                    copies.append(pltpu.make_async_copy(source, sink, w_sem.at[slot, len(copies)]))
        return copies

    def token_copies(at):
        lanes = slice(at * chunk, at * chunk + chunk)
        pairs = (
            (rims_ref.at[0:HALO, lanes], tok_s.at[0:HALO, lanes]),
            (own_ref.at[:, lanes], tok_s.at[HALO:pitch, lanes]),
            (rims_ref.at[HALO : 2 * HALO, lanes], tok_s.at[pitch : pitch + HALO, lanes]),
            (other_ref.at[:, lanes], tok_s.at[pitch + HALO : 2 * pitch, lanes]),
        )
        return [
            pltpu.make_async_copy(source, sink, tok_sem.at[at, place])
            for place, (source, sink) in enumerate(pairs)
        ]

    @pl.when(step == 0)
    def _():
        for copy in weight_copies(0):
            copy.start()
        for at in range(CHUNKS):
            for copy in token_copies(at):
                copy.start()
        for copy in weight_copies(1):
            copy.start()
        for copy in weight_copies(0):
            copy.wait()

    for at in range(1, steps):

        @pl.when(step == at)
        def _(at=at):
            if at + 1 < steps:
                for copy in weight_copies(at + 1):
                    copy.start()
            for copy in weight_copies(at):
                copy.wait()

    def convolve(request):
        taps = conv_ref.shape[0]
        total = None
        for tap in range(taps):
            start = request * pitch + HALO - taps + 1 + tap
            part = raw_s[pl.ds(start, count), :] * conv_ref[tap : tap + 1, :]
            total = part if total is None else total + part
        return total

    @pl.when(step == 0)
    def _():
        planes = 8 // CHUNKS
        both = None
        for at in range(CHUNKS):
            for copy in token_copies(at):
                copy.wait()
            token = tok_s[:, at * chunk : at * chunk + chunk]
            main = dot(token, w_s[0, at * planes : (at + 1) * planes].reshape(chunk, WIDE))
            small = dot(token, small_s[at * planes : (at + 1) * planes].reshape(chunk, 128))
            if at == 0:
                proj_s[...] = main
                raw_s[:, :128] = small
            else:
                proj_s[...] += main
                raw_s[:, :128] += small
        row = lax.broadcasted_iota(jnp.int32, (count, count), 0)
        col = lax.broadcasted_iota(jnp.int32, (count, count), 1)
        lower = jnp.where(col <= row, 1.0, 0.0).astype(BF16)
        for request in range(2):
            x = raw_s[pl.ds(request * pitch + HALO, count), :128]
            size = jnp.maximum(x, 0.0) + jnp.log1p(jnp.exp(-jnp.abs(x)))
            first, second, third = split_three(-size * rate_ref[...])
            sums = dot(lower, first) + dot(lower, second) + dot(lower, third)
            turned = sums.T
            for group in range(4):
                sums_t[request, group] = turned[4 * group : 4 * group + 8]
                sums_s[request, group] = sums if group == 0 else pltpu.roll(sums, 128 - 4 * group, 1)
            step_s[request, :, :128], step_s[request, :, 128:] = two_parts(size)
            fade = jnp.exp(sums[count - 1 :] - sums)
            fade_s[request, :, :128], fade_s[request, :, 128:] = two_parts(fade)
            grow_ref[request, :, :128], grow_ref[request, :, 128:] = two_parts(jnp.exp(sums))
            first, second, third = split_three(jnp.broadcast_to(sums[count - 1 :], (16, 128)))
            place = lax.broadcasted_iota(jnp.int32, (16, 128), 0)
            total = jnp.where(
                place == 0,
                first.astype(F32),
                jnp.where(
                    place == 1, second.astype(F32), jnp.where(place == 2, third.astype(F32), 0.0)
                ),
            )
            total_s[request] = total.astype(BF16)
        raw_s[...] = proj_s[...].astype(BF16).astype(F32)
        apart = (row >> 6) ^ (col >> 6)
        for request in range(2):
            mixed = convolve(request).astype(BF16)
            query = mixed[:, STATE:]
            query_ref[request] = query
            keys_t = mixed[:, :STATE].astype(F32).T.astype(BF16)
            keys_s[request] = keys_t
            weight = jnp.where(
                apart == 0,
                level_ref[request, 0],
                jnp.where(
                    apart == 1,
                    level_ref[request, 1],
                    jnp.where(apart < 4, level_ref[request, 2], level_ref[request, 3]),
                ),
            )
            score_s[request] = dot(query, keys_t) * jnp.where(col <= row, weight, 0.0)

    @pl.when(step >= 1)
    def _():
        raw_s[...] = dot(tok_s[...], w_s[step % 2].reshape(width, WIDE)).astype(BF16).astype(F32)
        lanes = spread(block, WIDE)
        for request in range(2):
            convolved = convolve(request)
            values = (convolved * jax.nn.sigmoid(convolved)).astype(BF16).astype(F32)
            driven = (values * dot(step_s[request], lanes)).astype(BF16)
            faded = (driven.astype(F32) * dot(fade_s[request], lanes)).astype(BF16)
            states = dot(keys_s[request], faded).astype(BF16)
            totals = dot(total_s[request], lanes[:128]).astype(BF16)
            for unit in range(4):
                pair, half = unit // 2, unit % 2
                cut = slice(pair * 128, pair * 128 + 128)
                send_ref[request, unit, :64] = states[half * 64 : half * 64 + 64, cut]
                send_ref[request, unit, 64:] = totals[:, cut]
            values_ref[request] = values.astype(BF16)
            driven_ref[request] = driven


def inner_kernel(values_ref, driven_ref, skip_ref, score_ref, sums_ref, turned_ref, part_ref):
    count = part_ref.shape[0]
    side = lax.broadcasted_iota(jnp.int32, (count, 128), 1) < 64
    for pair in range(2):
        cut = slice(pair * 128, pair * 128 + 128)
        both = driven_ref[0, :, cut]
        sides = (
            jnp.where(side, both, jnp.zeros_like(both)),
            jnp.where(side, jnp.zeros_like(both), both),
        )
        for tile in range(count // 128):
            top, reach = tile * 128, tile * 128 + 128
            total = values_ref[0, top:reach, cut].astype(F32) * skip_ref[:, cut]
            score = score_ref[0, top:reach, :reach]
            for half in range(2):
                head = 2 * pair + half
                later = sums_ref[0, 0, top:reach, head : head + 1]
                earlier = turned_ref[0, 0, head : head + 1, :reach]
                weight = score * jnp.exp(jnp.minimum(later - earlier, 0.0))
                total = total + dot(weight.astype(BF16), sides[half][:reach])
            part_ref[top:reach, cut] = total


def order_z_kernel(coord_ref, *refs):
    pieces, outs = refs[:9], refs[9:]
    for part in range(2):
        for place in range(7):
            outs[part][coord_ref[8 + place]] = pieces[place][part]
        outs[part][coord_ref[15]] = pieces[7 + part][0]


def order_kernel(base, coord_ref, *refs):
    pieces, out_ref = refs[:5], refs[5]
    half = out_ref.shape[0] // 2
    for place in range(3):
        out_ref[:, coord_ref[base + place]] = pieces[place][...]
    out_ref[:half, coord_ref[base + 3]] = pieces[3][...]
    out_ref[half:, coord_ref[base + 3]] = pieces[4][...]


def scan_kernel(coord_ref, level_ref, state_ref, out_ref, sum_s, block_s):
    count = state_ref.shape[0]
    request = coord_ref[17]
    totals = []
    for place in range(count):
        rows = state_ref[place, 64:80].astype(F32)
        totals.append(rows[0:1] + rows[1:2] + rows[2:3])
    before = [jnp.zeros_like(totals[0])]
    for place in range(count - 1):
        before.append(before[-1] + totals[place])
    sum_s[...] = jnp.zeros_like(sum_s)
    for place in range(count):
        block_s[place] = state_ref[place, :64].astype(F32)
    level = 0
    while (1 << level) < count:
        span = 1 << level
        for start in range(span, count, 2 * span):
            previous = block_s[start - span] * level_ref[request, 4 + level]
            for place in range(start, start + span):
                sum_s[place] += jnp.exp(before[place] - before[start]) * previous
            end = start + span
            gone = totals[start]
            for place in range(start + 1, end):
                gone = gone + totals[place]
            block_s[start - span] = block_s[start - span] * jnp.exp(gone) + block_s[start]
        level += 1
    out_ref[...] = sum_s[...].astype(BF16)


def finish_kernel(request, coord_ref, fact_ref, part_ref, state_ref, query_ref, grow_ref, out_ref):
    count = part_ref.shape[0]
    block = pl.program_id(0)
    grow = dot(grow_ref[0], spread(block, WIDE))
    first = lax.broadcasted_iota(jnp.int32, (128, 128), 0)
    second = lax.broadcasted_iota(jnp.int32, (128, 128), 1)
    ones = jnp.where((first >> 6) == (second >> 6), 1.0, 0.0).astype(BF16)
    spot = coord_ref[18] + lax.broadcasted_iota(jnp.int32, (count, 128), 0)
    live = spot < fact_ref[request, 11]
    for pair in range(2):
        lanes = slice(pair * 128, pair * 128 + 128)
        state = jnp.concatenate([state_ref[2 * pair], state_ref[2 * pair + 1]], 0)
        y = part_ref[:, lanes] + grow[:, lanes] * dot(query_ref[0], state)
        mean = dot((y * y).astype(BF16), ones) * (1.0 / 64.0)
        y = y * lax.rsqrt(mean + 1e-05)
        out_ref[:, lanes] = jnp.where(live, y, 0.0).astype(BF16)


def params():
    return pltpu.CompilerParams(dimension_semantics=("arbitrary",), vmem_limit_bytes=56 * 2**20)


ANY = pl.BlockSpec(memory_space=pl.ANY)
VMEM = pl.BlockSpec(memory_space=pltpu.VMEM)
SMEM = pl.BlockSpec(memory_space=pltpu.SMEM)


def near(i):
    return i ^ 1


def far(i):
    return ((i + 1) ^ 1) - 1


def along_z(value, move):
    return lax.ppermute(value, "seq", [(i, move(i // 4) % 8 * 4 + i % 4) for i in range(32)])


def along_x(value, move):
    return lax.ppermute(value, "seq", [(i, i // 4 * 4 + move(i % 4) % 4) for i in range(32)])


def along_y(value, move):
    return lax.ppermute(value, "dp", [(i, move(i // 2) % 4 * 2 + i % 2) for i in range(8)])


def to_twin(value):
    return lax.ppermute(value, "dp", [(i, i ^ 1) for i in range(8)])


def ring_of_four(value, along, extra=None):
    half = value.shape[0] // 2
    first = along(value, near)
    second = along(value, far)
    if extra is not None:
        second, extra = lax.optimization_barrier((second, extra))
    return extra, (value, first, second, along(second[:half], near), along(first[half:], far))


def ordered(pieces, coords, base, name):
    shape = pieces[0].shape
    return pl.pallas_call(
        lambda *refs: order_kernel(base, *refs),
        out_shape=jax.ShapeDtypeStruct((shape[0], 4) + shape[1:], BF16),
        in_specs=[SMEM] + [VMEM] * 5,
        out_specs=VMEM,
        name=name,
    )(coords, *pieces)


def gather_weights(w_in, core, coords, extra):
    depth = w_in.shape[0]
    tiles = w_in[:, :2304].reshape(depth, 18, 128).transpose(1, 0, 2)

    def share(of):
        small = lax.dynamic_slice(w_in, (0, 2304 + 16 * of), (depth, 16))
        small = jnp.pad(small, ((0, 0), (0, 112)))[None]
        return jnp.concatenate([tiles[16:], small, lax.dynamic_slice_in_dim(tiles, 8 * of, 8)], 0)

    mine = share(core)
    got = to_twin(share(1 - core))
    low = jnp.where(core == 0, mine, got)
    high = jnp.where(core == 0, got, mine)
    start = jnp.stack([low, high], 1).reshape(2, SHARE, 128)
    a1, b1 = along_z(start, near), along_z(start, far)
    a2, b2 = along_z(b1, near), along_z(a1, far)
    a3, b3 = along_z(b2, near), along_z(a2, far)
    a4, b4 = along_z(b3[:1], near), along_z(a3[1:], far)
    first, second = pl.pallas_call(
        order_z_kernel,
        out_shape=(jax.ShapeDtypeStruct((8, SHARE, 128), BF16),) * 2,
        in_specs=[SMEM] + [VMEM] * 9,
        out_specs=(VMEM, VMEM),
        name="order_z",
    )(coords, start, a1, b1, a2, b2, a3, b3, a4, b4)
    first = ordered(ring_of_four(first, along_x)[1], coords, 4, "order_x")
    second = ordered(ring_of_four(second, along_y)[1], coords, 0, "order_y")
    extra, back = ring_of_four(second, along_x, extra)
    _, front = ring_of_four(first, along_y)
    return extra, front + back


def body(tokens, w_in, conv_w, a_rate, d_skip, level_w, lengths):
    token_rows = tokens.reshape(-1, tokens.shape[-1])
    count, width = token_rows.shape
    taps, channels = conv_w.shape
    heads = a_rate.shape[0] // 2
    inner = (channels - 2 * STATE) // 2
    head_dim = inner // heads
    blocks = inner // WIDE
    ring = lax.axis_size("seq")
    position = lax.axis_index("seq")
    line = lax.axis_index("dp")
    core = line % 2
    y, x, z = line // 2, position % 4, position // 4

    def hop(i):
        return jnp.mod(((i + 1) ^ 1) - 1, 8)

    trail = [z, z ^ 1, hop(z)]
    trail += [hop(z ^ 1), hop(z) ^ 1]
    trail += [trail[4 - 1] ^ 1, hop(trail[4])]
    trail += [jnp.mod(z + 4, 8)]
    coords = jnp.stack(
        [y, y ^ 1, 3 - y, y ^ 2, x, x ^ 1, 3 - x, x ^ 2] + trail + [core * blocks, position // 16, position * count])
    coords = coords.astype(jnp.int32)

    other_rows = to_twin(token_rows)
    tails = jnp.stack([token_rows[count - taps + 1 :], other_rows[count - taps + 1 :]])
    rims = lax.ppermute(tails, "seq", [(i, i + 1) for i in range(ring - 1)])
    rims = jnp.pad(rims, ((0, 0), (HALO - taps + 1, 0), (0, 0))).reshape(2 * HALO, width)
    facts = jnp.concatenate([level_w.reshape(-1), lengths, jnp.zeros((4,), jnp.int32)])
    facts = jnp.stack([facts, to_twin(facts)])
    levels = facts.astype(F32) / 256.0

    rate = jnp.pad(lax.dynamic_slice(a_rate, (core * heads,), (heads,)), (0, 128 - heads))[None]
    skip = jnp.repeat(lax.dynamic_slice(d_skip, (core * heads,), (heads,)), head_dim)[None]
    conv = jnp.concatenate(
        [conv_w[:, 2 * inner :], lax.dynamic_slice(conv_w, (0, core * inner), (taps, inner))], 1
    )

    extra = (rims, other_rows, facts, levels, rate, skip, conv)
    extra, pieces = gather_weights(w_in, core, coords, extra)
    rims, other_rows, facts, levels, rate, skip, conv = extra

    def head_block(i):
        return jnp.maximum(i - 1, 0)

    values, driven, send, query, grow, score, sums, turned = pl.pallas_call(
        mix_kernel,
        out_shape=(
            jax.ShapeDtypeStruct((2, count, inner), BF16),
            jax.ShapeDtypeStruct((2, count, inner), BF16),
            jax.ShapeDtypeStruct((2, heads, ROWS, 128), BF16),
            jax.ShapeDtypeStruct((2, count, STATE), BF16),
            jax.ShapeDtypeStruct((2, count, 256), BF16),
            jax.ShapeDtypeStruct((2, count, count), F32),
            jax.ShapeDtypeStruct((2, blocks, count, 128), F32),
            jax.ShapeDtypeStruct((2, blocks, 8, count), F32),
        ),
        grid=(blocks + 1,),
        in_specs=[SMEM, SMEM]
        + [ANY] * 13
        + [
            pl.BlockSpec((taps, WIDE), lambda i: (0, i)),
            pl.BlockSpec((1, 128), lambda i: (0, 0)),
        ],
        out_specs=(
            pl.BlockSpec((2, count, WIDE), lambda i: (0, 0, head_block(i))),
            pl.BlockSpec((2, count, WIDE), lambda i: (0, 0, head_block(i))),
            pl.BlockSpec((2, 4, ROWS, 128), lambda i: (0, head_block(i), 0, 0)),
            pl.BlockSpec((2, count, STATE), lambda i: (0, 0, 0)),
            pl.BlockSpec((2, count, 256), lambda i: (0, 0, 0)),
            pl.BlockSpec((2, count, count), lambda i: (0, 0, 0)),
            pl.BlockSpec((2, blocks, count, 128), lambda i: (0, 0, 0, 0)),
            pl.BlockSpec((2, blocks, 8, count), lambda i: (0, 0, 0, 0)),
        ),
        scratch_shapes=[
            pltpu.VMEM((2 * (count + HALO), width), BF16),
            pltpu.VMEM((2, 8, 4, 4, 32, WIDE), BF16),
            pltpu.VMEM((8, 4, 4, 32, 128), BF16),
            pltpu.VMEM((2 * (count + HALO), WIDE), F32),
            pltpu.VMEM((2 * (count + HALO), WIDE), F32),
            pltpu.VMEM((2, STATE, count), BF16),
            pltpu.VMEM((2, count, 256), BF16),
            pltpu.VMEM((2, count, 256), BF16),
            pltpu.VMEM((2, 16, 128), BF16),
            pltpu.SemaphoreType.DMA((CHUNKS, 4)),
            pltpu.SemaphoreType.DMA((2, 15)),
        ],
        compiler_params=params(),
        name="mix",
    )(coords, levels, token_rows, other_rows, rims, *pieces, conv, rate)

    def inside(request):
        return pl.pallas_call(
            inner_kernel,
            out_shape=jax.ShapeDtypeStruct((count, inner), F32),
            grid=(blocks,),
            in_specs=[
                pl.BlockSpec((1, count, WIDE), lambda i: (request, 0, i)),
                pl.BlockSpec((1, count, WIDE), lambda i: (request, 0, i)),
                pl.BlockSpec((1, WIDE), lambda i: (0, i)),
                pl.BlockSpec((1, count, count), lambda i: (request, 0, 0)),
                pl.BlockSpec((1, 1, count, 128), lambda i: (request, i, 0, 0)),
                pl.BlockSpec((1, 1, 8, count), lambda i: (request, i, 0, 0)),
            ],
            out_specs=pl.BlockSpec((count, WIDE), lambda i: (0, i)),
            compiler_params=params(),
            cost_estimate=pl.CostEstimate(
                flops=10**10, transcendentals=3 * 10**6, bytes_accessed=6 * 10**6
            ),
            name="inner",
        )(values, driven, skip, score, sums, turned)


    gathered = lax.all_to_all(send.reshape(ring, ROWS, 128), "seq", 0, 0, tiled=True)
    later = inside(1)
    gathered, later = lax.optimization_barrier((gathered, later))
    scanned = pl.pallas_call(
        scan_kernel,
        out_shape=jax.ShapeDtypeStruct((ring, 64, 128), BF16),
        in_specs=[SMEM, SMEM, VMEM],
        out_specs=VMEM,
        scratch_shapes=[pltpu.VMEM((ring, 64, 128), F32), pltpu.VMEM((ring, 64, 128), F32)],
        compiler_params=pltpu.CompilerParams(vmem_limit_bytes=32 * 2**20),
        name="scan",
    )(coords, levels, gathered)
    carried = lax.all_to_all(scanned, "seq", 0, 0, tiled=True)
    carried, sooner = lax.optimization_barrier((carried, inside(0)))
    parts = (sooner, later)

    def finish(request, columns):
        return pl.pallas_call(
            lambda *refs: finish_kernel(request, *refs),
            out_shape=jax.ShapeDtypeStruct((count, columns), BF16),
            grid_spec=pltpu.PrefetchScalarGridSpec(
                num_scalar_prefetch=2,
                grid=(blocks,),
                in_specs=[
                    pl.BlockSpec((count, WIDE), lambda i, at, facts: (0, i)),
                    pl.BlockSpec((4, 64, 128), lambda i, at, facts: (4 * request + i, 0, 0)),
                    pl.BlockSpec((1, count, STATE), lambda i, at, facts: (request, 0, 0)),
                    pl.BlockSpec((1, count, 256), lambda i, at, facts: (request, 0, 0)),
                ],
                out_specs=pl.BlockSpec(
                    (count, WIDE),
                    lambda i, at, facts: (0, i if request else at[16] + i),
                ),
            ),
            compiler_params=params(),
            name="finish",
        )(coords, facts, parts[request], carried, query, grow)

    returned = to_twin(finish(1, inner))
    output = finish(0, 2 * inner)
    output = lax.dynamic_update_slice(output, returned, (0, (1 - core) * inner))
    return output.reshape(1, count, 2 * inner)


def solution(mesh):
    in_specs = (P("dp", "seq", None), P(("seq", "dp"), None), P(), P(), P(), P("dp", None), P("dp"))
    out_specs = P("dp", "seq", None)
    return jax.shard_map(body, mesh=mesh, in_specs=in_specs, out_specs=out_specs, check_vma=False)
```

```python
import jax
import jax.numpy as jnp
from jax import lax
from jax.experimental import pallas as pl
from jax.experimental.pallas import tpu as pltpu
from jax.sharding import PartitionSpec as P


STATE = 128
HALO = 16
WIDE = 256
ROWS = 72
UNIT = 16
SHARE = 11 * UNIT
CHUNKS = 8
SEGMENTS = (
    ((0, 0, 32, 0),),
    ((0, 32, 32, 0),),
    ((0, 64, 32, 0),),
    ((0, 96, 32, 0),),
    ((0, 128, 32, 0),),
    ((0, 160, 16, 0), (1, 0, 16, 16)),
) + tuple(((1, 16 + 32 * i, 32, 0),) for i in range(5))
F32 = jnp.float32
BF16 = jnp.bfloat16


def dot(a, b):
    return jnp.dot(a, b, preferred_element_type=F32)


def two_parts(x):
    high = x.astype(BF16)
    return high, (x - high.astype(F32)).astype(BF16)


def spread(block, width):
    head = lax.broadcasted_iota(jnp.int32, (2 * 128, width), 0) & 127
    lane = lax.broadcasted_iota(jnp.int32, (2 * 128, width), 1)
    return jnp.where(head == 4 * block + (lane >> 6), 1.0, 0.0).astype(BF16)


def split_three(x):
    first = x.astype(BF16)
    rest = x - first.astype(F32)
    second = rest.astype(BF16)
    return first, second, (rest - second.astype(F32)).astype(BF16)


def mix_kernel(
    coord_ref, own_ref, other_ref, rims_ref,
    a0, a1, a2, a3, a4, b0, b1, b2, b3, b4,
    conv_ref, rate_ref,
    values_ref, driven_ref, send_ref, query_ref, grow_ref, keys_ref, sums_s, sums_t,
    tok_s, w_s, small_s, proj_s, raw_a, raw_b, keys_s, step_s, fade_s, total_s,
    tok_sem, w_sem,
):
    count = own_ref.shape[0]
    pitch = count + HALO
    width = own_ref.shape[1]
    chunk = width // CHUNKS
    step = pl.program_id(0)
    steps = 5
    block = step - 1

    def weight_copies(at):
        slot = at % 2
        columns = (0, 1, 2) if at == 0 else (2 * at + 1, 2 * at + 2)
        copies = []
        for index, column in enumerate(columns):
            if column == 2:
                target, lanes = small_s, slice(0, 128)
            else:
                target, lanes = w_s.at[slot], slice(index * 128, index * 128 + 128)
            for part, row, rows, offset in SEGMENTS[column]:
                into = slice(offset, offset + rows)
                for piece, ref in enumerate(((a0, a1, a2, a3, a4), (b0, b1, b2, b3, b4))[part]):
                    planes = (slice(0, 8), slice(0, 8), slice(0, 8), slice(0, 4), slice(4, 8))[piece]
                    where = coord_ref[4 * part + min(piece, 3)]
                    source = ref.at[:, :, row : row + rows, :]
                    if part == 0:
                        sink = target.at[planes, :, where, into, lanes]
                    else:
                        sink = target.at[planes, where, :, into, lanes]
                    copies.append(pltpu.make_async_copy(source, sink, w_sem.at[slot, len(copies)]))
        return copies

    def token_copies(at):
        lanes = slice(at * chunk, at * chunk + chunk)
        pairs = (
            (rims_ref.at[0:HALO, lanes], tok_s.at[0:HALO, lanes]),
            (own_ref.at[:, lanes], tok_s.at[HALO:pitch, lanes]),
            (rims_ref.at[HALO : 2 * HALO, lanes], tok_s.at[pitch : pitch + HALO, lanes]),
            (other_ref.at[:, lanes], tok_s.at[pitch + HALO : 2 * pitch, lanes]),
        )
        return [
            pltpu.make_async_copy(source, sink, tok_sem.at[at, place])
            for place, (source, sink) in enumerate(pairs)
        ]

    @pl.when(step == 0)
    def _():
        for copy in weight_copies(0):
            copy.start()
        for at in range(CHUNKS):
            for copy in token_copies(at):
                copy.start()
        for copy in weight_copies(1):
            copy.start()
        for copy in weight_copies(0):
            copy.wait()

    def project(request, slot):
        rows = tok_s[request * pitch : request * pitch + pitch]
        return dot(rows, w_s[slot].reshape(width, WIDE)).astype(BF16).astype(F32)

    def convolve(source, base):
        taps = conv_ref.shape[0]
        total = None
        for tap in range(taps):
            start = base + HALO - taps + 1 + tap
            part = source[pl.ds(start, count), :] * conv_ref[tap : tap + 1, :]
            total = part if total is None else total + part
        return total

    @pl.when(step == 0)
    def _():
        planes = 8 // CHUNKS
        for at in range(CHUNKS):
            for copy in token_copies(at):
                copy.wait()
            token = tok_s[:, at * chunk : at * chunk + chunk]
            main = dot(token, w_s[0, at * planes : (at + 1) * planes].reshape(chunk, WIDE))
            small = dot(token, small_s[at * planes : (at + 1) * planes].reshape(chunk, 128))
            if at == 0:
                proj_s[...] = main
                raw_b[:, :128] = small[:pitch]
                raw_b[:, 128:] = small[pitch:]
            else:
                proj_s[...] += main
                raw_b[:, :128] += small[:pitch]
                raw_b[:, 128:] += small[pitch:]
        for copy in weight_copies(2):
            copy.start()
        for copy in weight_copies(1):
            copy.wait()
        raw_a[...] = project(0, 1)
        row = lax.broadcasted_iota(jnp.int32, (count, count), 0)
        col = lax.broadcasted_iota(jnp.int32, (count, count), 1)
        lower = jnp.where(col <= row, 1.0, 0.0).astype(BF16)
        for request in range(2):
            x = raw_b[pl.ds(HALO, count), 128 * request : 128 * request + 128]
            size = jnp.maximum(x, 0.0) + jnp.log1p(jnp.exp(-jnp.abs(x)))
            first, second, third = split_three(-size * rate_ref[...])
            sums = dot(lower, first) + dot(lower, second) + dot(lower, third)
            turned = sums.T
            for group in range(4):
                sums_t[request, group] = turned[4 * group : 4 * group + 8]
                sums_s[request, group] = sums if group == 0 else pltpu.roll(sums, 128 - 4 * group, 1)
            step_s[request, :, :128], step_s[request, :, 128:] = two_parts(size)
            fade = jnp.exp(sums[count - 1 :] - sums)
            fade_s[request, :, :128], fade_s[request, :, 128:] = two_parts(fade)
            grow_ref[request, :, :128], grow_ref[request, :, 128:] = two_parts(jnp.exp(sums))
            first, second, third = split_three(jnp.broadcast_to(sums[count - 1 :], (16, 128)))
            place = lax.broadcasted_iota(jnp.int32, (16, 128), 0)
            total = jnp.where(
                place == 0,
                first.astype(F32),
                jnp.where(
                    place == 1, second.astype(F32), jnp.where(place == 2, third.astype(F32), 0.0)
                ),
            )
            total_s[request] = total.astype(BF16)
        proj_s[...] = proj_s[...].astype(BF16).astype(F32)
        for request in range(2):
            mixed = convolve(proj_s, request * pitch).astype(BF16)
            query = mixed[:, STATE:]
            query_ref[request] = query
            keys_t = mixed[:, :STATE].astype(F32).T.astype(BF16)
            keys_s[request] = keys_t
            keys_ref[request] = keys_t

    def drive(request, source):
        lanes = spread(block, WIDE)
        convolved = convolve(source, 0)
        half = 0.5 * convolved
        values = (half + half * jnp.tanh(half)).astype(BF16)
        values_ref[request] = values
        driven = (values.astype(F32) * dot(step_s[request], lanes)).astype(BF16)
        driven_ref[request] = driven
        faded = (driven.astype(F32) * dot(fade_s[request], lanes)).astype(BF16)
        states = dot(keys_s[request], faded).astype(BF16)
        totals = dot(total_s[request], lanes[:128]).astype(BF16)
        for unit in range(4):
            pair, half = unit // 2, unit % 2
            cut = slice(pair * 128, pair * 128 + 128)
            send_ref[request, unit, :64] = states[half * 64 : half * 64 + 64, cut]
            send_ref[request, unit, 64:] = totals[: ROWS - 64, cut]

    @pl.when(step >= 1)
    def _():
        raw_b[...] = project(1, step % 2)
        drive(0, raw_a)

    for at in range(1, steps - 1):

        @pl.when(step == at)
        def _(at=at):
            if at + 2 < steps:
                for copy in weight_copies(at + 2):
                    copy.start()
            for copy in weight_copies(at + 1):
                copy.wait()

    @pl.when(step >= 1)
    def _():
        raw_a[...] = project(0, (step + 1) % 2)
        drive(1, raw_b)


def inner_kernel(
    request, level_ref, values_ref, driven_ref, skip_ref, query_ref, keys_ref, sums_ref, turned_ref,
    part_ref, score_s,
):
    count = part_ref.shape[0]

    @pl.when(pl.program_id(0) == 0)
    def _():
        row = lax.broadcasted_iota(jnp.int32, (count, count), 0)
        col = lax.broadcasted_iota(jnp.int32, (count, count), 1)
        apart = (row >> 6) ^ (col >> 6)
        weight = jnp.where(
            apart == 0,
            level_ref[request, 0],
            jnp.where(
                apart == 1,
                level_ref[request, 1],
                jnp.where(apart < 4, level_ref[request, 2], level_ref[request, 3]),
            ),
        )
        score_s[...] = dot(query_ref[0], keys_ref[0]) * jnp.where(col <= row, weight, 0.0)

    side = lax.broadcasted_iota(jnp.int32, (count, 128), 1) < 64
    for pair in range(2):
        cut = slice(pair * 128, pair * 128 + 128)
        both = driven_ref[0, :, cut]
        sides = (
            jnp.where(side, both, jnp.zeros_like(both)),
            jnp.where(side, jnp.zeros_like(both), both),
        )
        for tile in range(count // 128):
            top, reach = tile * 128, tile * 128 + 128
            total = values_ref[0, top:reach, cut].astype(F32) * skip_ref[:, cut]
            score = score_s[top:reach, :reach]
            for half in range(2):
                head = 2 * pair + half
                later = sums_ref[0, 0, top:reach, head : head + 1]
                earlier = turned_ref[0, 0, head : head + 1, :reach]
                weight = score * jnp.exp(jnp.minimum(later - earlier, 0.0))
                total = total + dot(weight.astype(BF16), sides[half][:reach])
            part_ref[top:reach, cut] = total.astype(BF16)


def order_z_kernel(coord_ref, *refs):
    pieces, outs = refs[:8], refs[8:]
    for part in range(2):
        for place in range(8):
            outs[part][coord_ref[8 + place]] = pieces[place][part]


def order_kernel(base, coord_ref, *refs):
    pieces, out_ref = refs[:4], refs[4]
    for place in range(4):
        out_ref[:, coord_ref[base + place]] = pieces[place][...]


def scan_kernel(coord_ref, level_ref, state_ref, out_ref, sum_s, block_s):
    count = state_ref.shape[0]
    request = coord_ref[17]
    totals = []
    for place in range(count):
        rows = state_ref[place, 64:ROWS].astype(F32)
        totals.append(rows[0:1] + rows[1:2] + rows[2:3])
    before = [jnp.zeros_like(totals[0])]
    for place in range(count - 1):
        before.append(before[-1] + totals[place])
    sum_s[...] = jnp.zeros_like(sum_s)
    for place in range(count):
        block_s[place] = state_ref[place, :64].astype(F32)
    level = 0
    while (1 << level) < count:
        span = 1 << level
        for start in range(span, count, 2 * span):
            previous = block_s[start - span] * level_ref[request, 4 + level]
            for place in range(start, start + span):
                sum_s[place] += jnp.exp(before[place] - before[start]) * previous
            end = start + span
            gone = totals[start]
            for place in range(start + 1, end):
                gone = gone + totals[place]
            block_s[start - span] = block_s[start - span] * jnp.exp(gone) + block_s[start]
        level += 1
    out_ref[...] = sum_s[...].astype(BF16)


def finish_kernel(request, coord_ref, fact_ref, part_ref, state_ref, query_ref, grow_ref, out_ref):
    count = part_ref.shape[0]
    block = pl.program_id(0)
    grow = dot(grow_ref[0], spread(2 * block, 2 * WIDE))
    first = lax.broadcasted_iota(jnp.int32, (128, 128), 0)
    second = lax.broadcasted_iota(jnp.int32, (128, 128), 1)
    ones = jnp.where((first >> 6) == (second >> 6), 1.0, 0.0).astype(BF16)
    spot = coord_ref[18] + lax.broadcasted_iota(jnp.int32, (count, 128), 0)
    live = spot < fact_ref[request, 11]
    for pair in range(4):
        lanes = slice(pair * 128, pair * 128 + 128)
        state = jnp.concatenate([state_ref[2 * pair], state_ref[2 * pair + 1]], 0)
        y = part_ref[:, lanes].astype(F32) + grow[:, lanes] * dot(query_ref[0], state)
        mean = dot((y * y).astype(BF16), ones) * (1.0 / 64.0)
        y = y * lax.rsqrt(mean + 1e-05)
        out_ref[:, lanes] = jnp.where(live, y, 0.0).astype(BF16)


def params():
    return pltpu.CompilerParams(dimension_semantics=("arbitrary",), vmem_limit_bytes=56 * 2**20)


ANY = pl.BlockSpec(memory_space=pl.ANY)
VMEM = pl.BlockSpec(memory_space=pltpu.VMEM)
SMEM = pl.BlockSpec(memory_space=pltpu.SMEM)


def near(i):
    return i ^ 1


def far(i):
    return ((i + 1) ^ 1) - 1


def along(value, axis, kind):
    pairs = []
    for i in range(256):
        place = {"z": i // 32, "x": i // 8 % 4, "y": i // 2 % 4}
        core = i % 2
        size = 8 if axis == "z" else 4
        move = near if core == kind else far
        place[axis] = move(place[axis]) % size
        pairs.append((i, ((place["z"] * 4 + place["x"]) * 4 + place["y"]) * 2 + core))
    return lax.ppermute(value, ("seq", "dp"), pairs)


def to_twin(value):
    return lax.ppermute(value, "dp", [(i, i ^ 1) for i in range(8)])


def ring_of_four(value, axis):
    first = along(value, axis, 0)
    second = along(value, axis, 1)
    return (value, first, second, along(second, axis, 0))


def halved_ring(value, axis, extra=None):
    half = value.shape[0] // 2
    first = along(value, axis, 0)
    second = along(value, axis, 1)
    if extra is not None:
        second, extra = lax.optimization_barrier((second, extra))
    return extra, (
        value, first, second, along(second[:half], axis, 0), along(first[half:], axis, 1)
    )


def ordered(pieces, coords, base, name):
    shape = pieces[0].shape
    return pl.pallas_call(
        lambda *refs: order_kernel(base, *refs),
        out_shape=jax.ShapeDtypeStruct((shape[0], 4) + shape[1:], BF16),
        in_specs=[SMEM] + [VMEM] * 4,
        out_specs=VMEM,
        name=name,
    )(coords, *pieces)


def gather_weights(w_in, core, coords, extra):
    depth = w_in.shape[0]
    tiles = w_in[:, :2304].reshape(depth, 18, 128).transpose(1, 0, 2)

    def share(of):
        small = lax.dynamic_slice(w_in, (0, 2304 + 16 * of), (depth, 16))
        small = jnp.pad(small, ((0, 0), (0, 112)))[None]
        return jnp.concatenate([tiles[16:], small, lax.dynamic_slice_in_dim(tiles, 8 * of, 8)], 0)

    mine = share(core)
    got = to_twin(share(1 - core))
    low = jnp.where(core == 0, mine, got)
    high = jnp.where(core == 0, got, mine)
    start = jnp.stack([low, high], 1).reshape(2, SHARE, 128)
    a1, b1 = along(start, "z", 0), along(start, "z", 1)
    a2, b2 = along(b1, "z", 0), along(a1, "z", 1)
    a3, b3 = along(b2, "z", 0), along(a2, "z", 1)
    a4 = along(b3, "z", 0)
    first, second = pl.pallas_call(
        order_z_kernel,
        out_shape=(jax.ShapeDtypeStruct((8, SHARE, 128), BF16),) * 2,
        in_specs=[SMEM] + [VMEM] * 8,
        out_specs=(VMEM, VMEM),
        name="order_z",
    )(coords, start, a1, b1, a2, b2, a3, b3, a4)
    first = ordered(ring_of_four(first, "x"), coords, 4, "order_x")
    second = ordered(ring_of_four(second, "y"), coords, 0, "order_y")
    rest, back = halved_ring(second, "x", extra(got))
    _, front = halved_ring(first, "y")
    return rest, front + back


def body(tokens, w_in, conv_w, a_rate, d_skip, level_w, lengths):
    token_rows = tokens.reshape(-1, tokens.shape[-1])
    count, width = token_rows.shape
    taps, channels = conv_w.shape
    heads = a_rate.shape[0] // 2
    inner = (channels - 2 * STATE) // 2
    head_dim = inner // heads
    blocks = inner // WIDE
    ring = lax.axis_size("seq")
    position = lax.axis_index("seq")
    line = lax.axis_index("dp")
    core = line % 2
    y, x, z = line // 2, position % 4, position // 4

    def one(i, size):
        return jnp.where(core == 0, i ^ 1, jnp.mod(((i + 1) ^ 1) - 1, size))

    def two(i, size):
        return jnp.where(core == 0, jnp.mod(((i + 1) ^ 1) - 1, size), i ^ 1)

    trail = [z, one(z, 8), two(z, 8)]
    trail += [two(trail[1], 8), one(trail[2], 8)]
    trail += [one(trail[3], 8), two(trail[4], 8), jnp.mod(z + 4, 8)]
    coords = jnp.stack(
        [y, one(y, 4), two(y, 4), y ^ 2, x, one(x, 4), two(x, 4), x ^ 2]
        + trail
        + [core * blocks // 2, position // 16, position * count]
    )
    coords = coords.astype(jnp.int32)

    def extra(got):
        rows, _ = lax.optimization_barrier((token_rows, got))
        other_rows = to_twin(rows)
        tails = jnp.stack([token_rows[count - taps + 1 :], other_rows[count - taps + 1 :]])
        rims = lax.ppermute(tails, "seq", [(i, i + 1) for i in range(ring - 1)])
        rims = jnp.pad(rims, ((0, 0), (HALO - taps + 1, 0), (0, 0))).reshape(2 * HALO, width)
        facts = jnp.concatenate([level_w.reshape(-1), lengths, jnp.zeros((4,), jnp.int32)])
        facts = jnp.stack([facts, to_twin(facts)])
        levels = facts.astype(F32) / 256.0
        rate = jnp.pad(lax.dynamic_slice(a_rate, (core * heads,), (heads,)), (0, 128 - heads))
        skip = jnp.repeat(lax.dynamic_slice(d_skip, (core * heads,), (heads,)), head_dim)
        own_conv = lax.dynamic_slice(conv_w, (0, core * inner), (taps, inner))
        conv = jnp.concatenate([conv_w[:, 2 * inner :], own_conv], 1)
        return rims, other_rows, facts, levels, rate[None], skip[None], conv

    rest, pieces = gather_weights(w_in, core, coords, extra)
    rims, other_rows, facts, levels, rate, skip, conv = rest

    def head_block(i):
        return jnp.maximum(i - 1, 0)

    values, driven, send, query, grow, keys, sums, turned = pl.pallas_call(
        mix_kernel,
        out_shape=(
            jax.ShapeDtypeStruct((2, count, inner), BF16),
            jax.ShapeDtypeStruct((2, count, inner), BF16),
            jax.ShapeDtypeStruct((2, heads, ROWS, 128), BF16),
            jax.ShapeDtypeStruct((2, count, STATE), BF16),
            jax.ShapeDtypeStruct((2, count, 256), BF16),
            jax.ShapeDtypeStruct((2, STATE, count), BF16),
            jax.ShapeDtypeStruct((2, blocks, count, 128), F32),
            jax.ShapeDtypeStruct((2, blocks, 8, count), F32),
        ),
        grid=(blocks + 1,),
        in_specs=[SMEM]
        + [ANY] * 13
        + [
            pl.BlockSpec((taps, WIDE), lambda i: (0, i)),
            pl.BlockSpec((1, 128), lambda i: (0, 0)),
        ],
        out_specs=(
            pl.BlockSpec((2, count, WIDE), lambda i: (0, 0, head_block(i))),
            pl.BlockSpec((2, count, WIDE), lambda i: (0, 0, head_block(i))),
            pl.BlockSpec((2, 4, ROWS, 128), lambda i: (0, head_block(i), 0, 0)),
            pl.BlockSpec((2, count, STATE), lambda i: (0, 0, 0)),
            pl.BlockSpec((2, count, 256), lambda i: (0, 0, 0)),
            pl.BlockSpec((2, STATE, count), lambda i: (0, 0, 0)),
            pl.BlockSpec((2, blocks, count, 128), lambda i: (0, 0, 0, 0)),
            pl.BlockSpec((2, blocks, 8, count), lambda i: (0, 0, 0, 0)),
        ),
        scratch_shapes=[
            pltpu.VMEM((2 * (count + HALO), width), BF16),
            pltpu.VMEM((2, 8, 4, 4, 32, WIDE), BF16),
            pltpu.VMEM((8, 4, 4, 32, 128), BF16),
            pltpu.VMEM((2 * (count + HALO), WIDE), F32),
            pltpu.VMEM((count + HALO, WIDE), F32),
            pltpu.VMEM((count + HALO, WIDE), F32),
            pltpu.VMEM((2, STATE, count), BF16),
            pltpu.VMEM((2, count, 256), BF16),
            pltpu.VMEM((2, count, 256), BF16),
            pltpu.VMEM((2, 16, 128), BF16),
            pltpu.SemaphoreType.DMA((CHUNKS, 4)),
            pltpu.SemaphoreType.DMA((2, 15)),
        ],
        compiler_params=params(),
        name="mix",
    )(coords, token_rows, other_rows, rims, *pieces, conv, rate)

    def inside(request):
        return pl.pallas_call(
            lambda *refs: inner_kernel(request, *refs),
            out_shape=jax.ShapeDtypeStruct((count, inner), BF16),
            grid=(blocks,),
            in_specs=[
                SMEM,
                pl.BlockSpec((1, count, WIDE), lambda i: (request, 0, i)),
                pl.BlockSpec((1, count, WIDE), lambda i: (request, 0, i)),
                pl.BlockSpec((1, WIDE), lambda i: (0, i)),
                pl.BlockSpec((1, count, STATE), lambda i: (request, 0, 0)),
                pl.BlockSpec((1, STATE, count), lambda i: (request, 0, 0)),
                pl.BlockSpec((1, 1, count, 128), lambda i: (request, i, 0, 0)),
                pl.BlockSpec((1, 1, 8, count), lambda i: (request, i, 0, 0)),
            ],
            out_specs=pl.BlockSpec((count, WIDE), lambda i: (0, i)),
            scratch_shapes=[pltpu.VMEM((count, count), F32)],
            compiler_params=params(),
            cost_estimate=pl.CostEstimate(
                flops=10**10, transcendentals=3 * 10**6, bytes_accessed=6 * 10**6
            ),
            name="inner",
        )(levels, values, driven, skip, query, keys, sums, turned)


    gathered = lax.all_to_all(send.reshape(ring, ROWS, 128), "seq", 0, 0, tiled=True)
    later = inside(1)
    gathered, later = lax.optimization_barrier((gathered, later))
    scanned = pl.pallas_call(
        scan_kernel,
        out_shape=jax.ShapeDtypeStruct((ring, 64, 128), BF16),
        in_specs=[SMEM, SMEM, VMEM],
        out_specs=VMEM,
        scratch_shapes=[pltpu.VMEM((ring, 64, 128), F32), pltpu.VMEM((ring, 64, 128), F32)],
        compiler_params=pltpu.CompilerParams(vmem_limit_bytes=32 * 2**20),
        name="scan",
    )(coords, levels, gathered)
    carried = lax.all_to_all(scanned, "seq", 0, 0, tiled=True)
    carried, sooner = lax.optimization_barrier((carried, inside(0)))
    parts = (sooner, later)

    def finish(request, columns):
        return pl.pallas_call(
            lambda *refs: finish_kernel(request, *refs),
            out_shape=jax.ShapeDtypeStruct((count, columns), BF16),
            grid_spec=pltpu.PrefetchScalarGridSpec(
                num_scalar_prefetch=2,
                grid=(blocks // 2,),
                in_specs=[
                    pl.BlockSpec((count, 2 * WIDE), lambda i, at, facts: (0, i)),
                    pl.BlockSpec((8, 64, 128), lambda i, at, facts: (2 * request + i, 0, 0)),
                    pl.BlockSpec((1, count, STATE), lambda i, at, facts: (request, 0, 0)),
                    pl.BlockSpec((1, count, 256), lambda i, at, facts: (request, 0, 0)),
                ],
                out_specs=pl.BlockSpec(
                    (count, 2 * WIDE),
                    lambda i, at, facts: (0, i if request else at[16] + i),
                ),
            ),
            compiler_params=params(),
            name="finish",
        )(coords, facts, parts[request], carried, query, grow)

    returned = to_twin(finish(1, inner))
    output = finish(0, 2 * inner)
    output = lax.dynamic_update_slice(output, returned, (0, (1 - core) * inner))
    return output.reshape(1, count, 2 * inner)


def solution(mesh):
    in_specs = (P("dp", "seq", None), P(("seq", "dp"), None), P(), P(), P(), P("dp", None), P("dp"))
    out_specs = P("dp", "seq", None)
    return jax.shard_map(body, mesh=mesh, in_specs=in_specs, out_specs=out_specs, check_vma=False)
```

```python
import jax
import jax.numpy as jnp
from jax import lax
from jax.experimental import pallas as pl
from jax.experimental.pallas import tpu as pltpu
from jax.sharding import PartitionSpec as P


STATE = 128
HALO = 16
WIDE = 256
ROWS = 72
UNIT = 16
SHARE = 11 * UNIT
CHUNKS = 8
SEGMENTS = (
    ((0, 0, 32, 0),),
    ((0, 32, 32, 0),),
    ((0, 64, 32, 0),),
    ((0, 96, 32, 0),),
    ((0, 128, 32, 0),),
    ((0, 160, 16, 0), (1, 0, 16, 16)),
) + tuple(((1, 16 + 32 * i, 32, 0),) for i in range(5))
F32 = jnp.float32
BF16 = jnp.bfloat16


def dot(a, b):
    return jnp.dot(a, b, preferred_element_type=F32)


def two_parts(x):
    high = x.astype(BF16)
    return high, (x - high.astype(F32)).astype(BF16)


def spread(block, width):
    head = lax.broadcasted_iota(jnp.int32, (2 * 128, width), 0) & 127
    lane = lax.broadcasted_iota(jnp.int32, (2 * 128, width), 1)
    return jnp.where(head == 4 * block + (lane >> 6), 1.0, 0.0).astype(BF16)


def split_three(x):
    first = x.astype(BF16)
    rest = x - first.astype(F32)
    second = rest.astype(BF16)
    return first, second, (rest - second.astype(F32)).astype(BF16)


def mix_kernel(
    coord_ref, own_ref, other_ref, rims_ref,
    a0, a1, a2, a3, a4, b0, b1, b2, b3, b4,
    conv_ref, rate_ref,
    values_ref, driven_ref, send_ref, query_ref, grow_ref, keys_ref, sums_s, sums_t,
    tok_s, w_s, small_s, proj_s, raw_a, raw_b, keys_s, step_s, fade_s, total_s,
    tok_sem, w_sem,
):
    count = own_ref.shape[0]
    pitch = count + HALO
    width = own_ref.shape[1]
    chunk = width // CHUNKS
    step = pl.program_id(0)
    steps = 5
    block = step - 1

    def weight_copies(at):
        slot = at % 2
        columns = (0, 1, 2) if at == 0 else (2 * at + 1, 2 * at + 2)
        copies = []
        for index, column in enumerate(columns):
            if column == 2:
                target, lanes = small_s, slice(0, 128)
            else:
                target, lanes = w_s.at[slot], slice(index * 128, index * 128 + 128)
            for part, row, rows, offset in SEGMENTS[column]:
                into = slice(offset, offset + rows)
                for piece, ref in enumerate(((a0, a1, a2, a3, a4), (b0, b1, b2, b3, b4))[part]):
                    planes = (slice(0, 8), slice(0, 8), slice(0, 8), slice(0, 4), slice(4, 8))[piece]
                    where = coord_ref[4 * part + min(piece, 3)]
                    source = ref.at[:, :, row : row + rows, :]
                    if part == 0:
                        sink = target.at[planes, :, where, into, lanes]
                    else:
                        sink = target.at[planes, where, :, into, lanes]
                    copies.append(pltpu.make_async_copy(source, sink, w_sem.at[slot, len(copies)]))
        return copies

    def token_copies(at):
        lanes = slice(at * chunk, at * chunk + chunk)
        pairs = (
            (rims_ref.at[0:HALO, lanes], tok_s.at[0:HALO, lanes]),
            (own_ref.at[:, lanes], tok_s.at[HALO:pitch, lanes]),
            (rims_ref.at[HALO : 2 * HALO, lanes], tok_s.at[pitch : pitch + HALO, lanes]),
            (other_ref.at[:, lanes], tok_s.at[pitch + HALO : 2 * pitch, lanes]),
        )
        return [
            pltpu.make_async_copy(source, sink, tok_sem.at[at, place])
            for place, (source, sink) in enumerate(pairs)
        ]

    @pl.when(step == 0)
    def _():
        for copy in weight_copies(0):
            copy.start()
        for at in range(CHUNKS):
            for copy in token_copies(at):
                copy.start()
        for copy in weight_copies(1):
            copy.start()
        for copy in weight_copies(0):
            copy.wait()

    def project(request, slot):
        rows = tok_s[request * pitch : request * pitch + pitch]
        return dot(rows, w_s[slot].reshape(width, WIDE)).astype(BF16).astype(F32)

    def convolve(raw):
        taps = conv_ref.shape[0]
        total = None
        for tap in range(taps):
            late = taps - 1 - tap
            moved = raw if late == 0 else pltpu.roll(raw, late, 0)
            part = moved[HALO:] * conv_ref[tap : tap + 1, :]
            total = part if total is None else total + part
        return total

    @pl.when(step == 0)
    def _():
        planes = 8 // CHUNKS
        for at in range(CHUNKS):
            for copy in token_copies(at):
                copy.wait()
            token = tok_s[:, at * chunk : at * chunk + chunk]
            main = dot(token, w_s[0, at * planes : (at + 1) * planes].reshape(chunk, WIDE))
            small = dot(token, small_s[at * planes : (at + 1) * planes].reshape(chunk, 128))
            if at == 0:
                proj_s[...] = main
                raw_b[:, :128] = small[:pitch]
                raw_b[:, 128:] = small[pitch:]
            else:
                proj_s[...] += main
                raw_b[:, :128] += small[:pitch]
                raw_b[:, 128:] += small[pitch:]
        for copy in weight_copies(2):
            copy.start()
        for copy in weight_copies(1):
            copy.wait()
        raw_a[...] = project(0, 1)
        row = lax.broadcasted_iota(jnp.int32, (count, count), 0)
        col = lax.broadcasted_iota(jnp.int32, (count, count), 1)
        lower = jnp.where(col <= row, 1.0, 0.0).astype(BF16)
        for request in range(2):
            x = raw_b[pl.ds(HALO, count), 128 * request : 128 * request + 128]
            size = jnp.maximum(x, 0.0) + jnp.log1p(jnp.exp(-jnp.abs(x)))
            first, second, third = split_three(-size * rate_ref[...])
            sums = dot(lower, first) + dot(lower, second) + dot(lower, third)
            turned = sums.T
            for group in range(4):
                sums_t[request, group] = turned[4 * group : 4 * group + 8]
                sums_s[request, group] = sums if group == 0 else pltpu.roll(sums, 128 - 4 * group, 1)
            step_s[request, :, :128], step_s[request, :, 128:] = two_parts(size)
            fade = jnp.exp(sums[count - 1 :] - sums)
            fade_s[request, :, :128], fade_s[request, :, 128:] = two_parts(fade)
            grow_ref[request, :, :128], grow_ref[request, :, 128:] = two_parts(jnp.exp(sums))
            first, second, third = split_three(jnp.broadcast_to(sums[count - 1 :], (16, 128)))
            place = lax.broadcasted_iota(jnp.int32, (16, 128), 0)
            total = jnp.where(
                place == 0,
                first.astype(F32),
                jnp.where(
                    place == 1, second.astype(F32), jnp.where(place == 2, third.astype(F32), 0.0)
                ),
            )
            total_s[request] = total.astype(BF16)
        proj_s[...] = proj_s[...].astype(BF16).astype(F32)
        for request in range(2):
            mixed = convolve(proj_s[request * pitch : request * pitch + pitch]).astype(BF16)
            query = mixed[:, STATE:]
            query_ref[request] = query
            keys_t = mixed[:, :STATE].astype(F32).T.astype(BF16)
            keys_s[request] = keys_t
            keys_ref[request] = keys_t

    def drive(request, source):
        lanes = spread(block, WIDE)
        convolved = convolve(source[...])
        half = 0.5 * convolved
        values = (half + half * jnp.tanh(half)).astype(BF16)
        values_ref[request] = values
        driven = (values.astype(F32) * dot(step_s[request], lanes)).astype(BF16)
        driven_ref[request] = driven
        faded = (driven.astype(F32) * dot(fade_s[request], lanes)).astype(BF16)
        states = dot(keys_s[request], faded).astype(BF16)
        totals = dot(total_s[request], lanes[:128]).astype(BF16)
        for unit in range(4):
            pair, half = unit // 2, unit % 2
            cut = slice(pair * 128, pair * 128 + 128)
            send_ref[request, unit, :64] = states[half * 64 : half * 64 + 64, cut]
            send_ref[request, unit, 64:] = totals[: ROWS - 64, cut]

    @pl.when(step >= 1)
    def _():
        raw_b[...] = project(1, step % 2)
        drive(0, raw_a)

    for at in range(1, steps - 1):

        @pl.when(step == at)
        def _(at=at):
            if at + 2 < steps:
                for copy in weight_copies(at + 2):
                    copy.start()
            for copy in weight_copies(at + 1):
                copy.wait()

    @pl.when(step >= 1)
    def _():
        raw_a[...] = project(0, (step + 1) % 2)
        drive(1, raw_b)


def inner_kernel(
    request, level_ref, values_ref, driven_ref, skip_ref, query_ref, keys_ref, sums_ref, turned_ref,
    part_ref, score_s,
):
    count = part_ref.shape[0]

    @pl.when(pl.program_id(0) == 0)
    def _():
        row = lax.broadcasted_iota(jnp.int32, (count, count), 0)
        col = lax.broadcasted_iota(jnp.int32, (count, count), 1)
        apart = (row >> 6) ^ (col >> 6)
        weight = jnp.where(
            apart == 0,
            level_ref[request, 0],
            jnp.where(
                apart == 1,
                level_ref[request, 1],
                jnp.where(apart < 4, level_ref[request, 2], level_ref[request, 3]),
            ),
        )
        score_s[...] = dot(query_ref[0], keys_ref[0]) * jnp.where(col <= row, weight, 0.0)

    side = lax.broadcasted_iota(jnp.int32, (count, 128), 1) < 64
    for pair in range(2):
        cut = slice(pair * 128, pair * 128 + 128)
        both = driven_ref[0, :, cut]
        sides = (
            jnp.where(side, both, jnp.zeros_like(both)),
            jnp.where(side, jnp.zeros_like(both), both),
        )
        for tile in range(count // 128):
            top, reach = tile * 128, tile * 128 + 128
            total = values_ref[0, top:reach, cut].astype(F32) * skip_ref[:, cut]
            score = score_s[top:reach, :reach]
            for half in range(2):
                head = 2 * pair + half
                later = sums_ref[0, 0, top:reach, head : head + 1]
                earlier = turned_ref[0, 0, head : head + 1, :reach]
                weight = score * jnp.exp(jnp.minimum(later - earlier, 0.0))
                total = total + dot(weight.astype(BF16), sides[half][:reach])
            part_ref[top:reach, cut] = total.astype(BF16)


def order_z_kernel(coord_ref, *refs):
    pieces, outs = refs[:8], refs[8:]
    for part in range(2):
        for place in range(8):
            outs[part][coord_ref[8 + place]] = pieces[place][part]


def order_kernel(base, coord_ref, *refs):
    pieces, out_ref = refs[:4], refs[4]
    for place in range(4):
        out_ref[:, coord_ref[base + place]] = pieces[place][...]


def scan_kernel(coord_ref, level_ref, state_ref, out_ref, sum_s, block_s):
    count = state_ref.shape[0]
    request = coord_ref[17]
    totals = []
    for place in range(count):
        rows = state_ref[place, 64:ROWS].astype(F32)
        totals.append(rows[0:1] + rows[1:2] + rows[2:3])
    before = [jnp.zeros_like(totals[0])]
    for place in range(count - 1):
        before.append(before[-1] + totals[place])
    sum_s[...] = jnp.zeros_like(sum_s)
    for place in range(count):
        block_s[place] = state_ref[place, :64].astype(F32)
    level = 0
    while (1 << level) < count:
        span = 1 << level
        for start in range(span, count, 2 * span):
            previous = block_s[start - span] * level_ref[request, 4 + level]
            for place in range(start, start + span):
                sum_s[place] += jnp.exp(before[place] - before[start]) * previous
            end = start + span
            gone = totals[start]
            for place in range(start + 1, end):
                gone = gone + totals[place]
            block_s[start - span] = block_s[start - span] * jnp.exp(gone) + block_s[start]
        level += 1
    out_ref[...] = sum_s[...].astype(BF16)


def finish_kernel(request, coord_ref, fact_ref, part_ref, state_ref, query_ref, grow_ref, out_ref):
    count = part_ref.shape[0]
    block = pl.program_id(0)
    grow = dot(grow_ref[0], spread(2 * block, 2 * WIDE))
    first = lax.broadcasted_iota(jnp.int32, (128, 128), 0)
    second = lax.broadcasted_iota(jnp.int32, (128, 128), 1)
    ones = jnp.where((first >> 6) == (second >> 6), 1.0, 0.0).astype(BF16)
    spot = coord_ref[18] + lax.broadcasted_iota(jnp.int32, (count, 128), 0)
    live = spot < fact_ref[request, 11]
    for pair in range(4):
        lanes = slice(pair * 128, pair * 128 + 128)
        state = jnp.concatenate([state_ref[2 * pair], state_ref[2 * pair + 1]], 0)
        y = part_ref[:, lanes].astype(F32) + grow[:, lanes] * dot(query_ref[0], state)
        mean = dot((y * y).astype(BF16), ones) * (1.0 / 64.0)
        y = y * lax.rsqrt(mean + 1e-05)
        out_ref[:, lanes] = jnp.where(live, y, 0.0).astype(BF16)


def params():
    return pltpu.CompilerParams(dimension_semantics=("arbitrary",), vmem_limit_bytes=56 * 2**20)


ANY = pl.BlockSpec(memory_space=pl.ANY)
VMEM = pl.BlockSpec(memory_space=pltpu.VMEM)
SMEM = pl.BlockSpec(memory_space=pltpu.SMEM)


def near(i):
    return i ^ 1


def far(i):
    return ((i + 1) ^ 1) - 1


def along(value, axis, kind):
    pairs = []
    for i in range(256):
        place = {"z": i // 32, "x": i // 8 % 4, "y": i // 2 % 4}
        core = i % 2
        size = 8 if axis == "z" else 4
        move = near if core == kind else far
        place[axis] = move(place[axis]) % size
        pairs.append((i, ((place["z"] * 4 + place["x"]) * 4 + place["y"]) * 2 + core))
    return lax.ppermute(value, ("seq", "dp"), pairs)


def to_twin(value):
    return lax.ppermute(value, "dp", [(i, i ^ 1) for i in range(8)])


def ring_of_four(value, axis):
    first = along(value, axis, 0)
    second = along(value, axis, 1)
    return (value, first, second, along(second, axis, 0))


def halved_ring(value, axis, extra=None):
    half = value.shape[0] // 2
    first = along(value, axis, 0)
    second = along(value, axis, 1)
    if extra is not None:
        second, extra = lax.optimization_barrier((second, extra))
    return extra, (
        value, first, second, along(second[:half], axis, 0), along(first[half:], axis, 1)
    )


def ordered(pieces, coords, base, name):
    shape = pieces[0].shape
    return pl.pallas_call(
        lambda *refs: order_kernel(base, *refs),
        out_shape=jax.ShapeDtypeStruct((shape[0], 4) + shape[1:], BF16),
        in_specs=[SMEM] + [VMEM] * 4,
        out_specs=VMEM,
        name=name,
    )(coords, *pieces)


def gather_weights(w_in, core, coords, extra):
    depth = w_in.shape[0]
    tiles = w_in[:, :2304].reshape(depth, 18, 128).transpose(1, 0, 2)

    def share(of):
        small = lax.dynamic_slice(w_in, (0, 2304 + 16 * of), (depth, 16))
        small = jnp.pad(small, ((0, 0), (0, 112)))[None]
        return jnp.concatenate([tiles[16:], small, lax.dynamic_slice_in_dim(tiles, 8 * of, 8)], 0)

    mine = share(core)
    got = to_twin(share(1 - core))
    low = jnp.where(core == 0, mine, got)
    high = jnp.where(core == 0, got, mine)
    start = jnp.stack([low, high], 1).reshape(2, SHARE, 128)
    a1, b1 = along(start, "z", 0), along(start, "z", 1)
    a2, b2 = along(b1, "z", 0), along(a1, "z", 1)
    a3, b3 = along(b2, "z", 0), along(a2, "z", 1)
    a4 = along(b3, "z", 0)
    first, second = pl.pallas_call(
        order_z_kernel,
        out_shape=(jax.ShapeDtypeStruct((8, SHARE, 128), BF16),) * 2,
        in_specs=[SMEM] + [VMEM] * 8,
        out_specs=(VMEM, VMEM),
        name="order_z",
    )(coords, start, a1, b1, a2, b2, a3, b3, a4)
    first = ordered(ring_of_four(first, "x"), coords, 4, "order_x")
    second = ordered(ring_of_four(second, "y"), coords, 0, "order_y")
    rest, back = halved_ring(second, "x", extra(got))
    _, front = halved_ring(first, "y")
    return rest, front + back


def body(tokens, w_in, conv_w, a_rate, d_skip, level_w, lengths):
    token_rows = tokens.reshape(-1, tokens.shape[-1])
    count, width = token_rows.shape
    taps, channels = conv_w.shape
    heads = a_rate.shape[0] // 2
    inner = (channels - 2 * STATE) // 2
    head_dim = inner // heads
    blocks = inner // WIDE
    ring = lax.axis_size("seq")
    position = lax.axis_index("seq")
    line = lax.axis_index("dp")
    core = line % 2
    y, x, z = line // 2, position % 4, position // 4

    def one(i, size):
        return jnp.where(core == 0, i ^ 1, jnp.mod(((i + 1) ^ 1) - 1, size))

    def two(i, size):
        return jnp.where(core == 0, jnp.mod(((i + 1) ^ 1) - 1, size), i ^ 1)

    trail = [z, one(z, 8), two(z, 8)]
    trail += [two(trail[1], 8), one(trail[2], 8)]
    trail += [one(trail[3], 8), two(trail[4], 8), jnp.mod(z + 4, 8)]
    coords = jnp.stack(
        [y, one(y, 4), two(y, 4), y ^ 2, x, one(x, 4), two(x, 4), x ^ 2]
        + trail
        + [core * blocks // 2, position // 16, position * count]
    )
    coords = coords.astype(jnp.int32)

    def extra(got):
        rows, _ = lax.optimization_barrier((token_rows, got))
        other_rows = to_twin(rows)
        tails = jnp.stack([token_rows[count - taps + 1 :], other_rows[count - taps + 1 :]])
        rims = lax.ppermute(tails, "seq", [(i, i + 1) for i in range(ring - 1)])
        rims = jnp.pad(rims, ((0, 0), (HALO - taps + 1, 0), (0, 0))).reshape(2 * HALO, width)
        facts = jnp.concatenate([level_w.reshape(-1), lengths, jnp.zeros((4,), jnp.int32)])
        facts = jnp.stack([facts, to_twin(facts)])
        levels = facts.astype(F32) / 256.0
        rate = jnp.pad(lax.dynamic_slice(a_rate, (core * heads,), (heads,)), (0, 128 - heads))
        skip = jnp.repeat(lax.dynamic_slice(d_skip, (core * heads,), (heads,)), head_dim)
        own_conv = lax.dynamic_slice(conv_w, (0, core * inner), (taps, inner))
        conv = jnp.concatenate([conv_w[:, 2 * inner :], own_conv], 1)
        return rims, other_rows, facts, levels, rate[None], skip[None], conv

    rest, pieces = gather_weights(w_in, core, coords, extra)
    rims, other_rows, facts, levels, rate, skip, conv = rest

    def head_block(i):
        return jnp.maximum(i - 1, 0)

    values, driven, send, query, grow, keys, sums, turned = pl.pallas_call(
        mix_kernel,
        out_shape=(
            jax.ShapeDtypeStruct((2, count, inner), BF16),
            jax.ShapeDtypeStruct((2, count, inner), BF16),
            jax.ShapeDtypeStruct((2, heads, ROWS, 128), BF16),
            jax.ShapeDtypeStruct((2, count, STATE), BF16),
            jax.ShapeDtypeStruct((2, count, 256), BF16),
            jax.ShapeDtypeStruct((2, STATE, count), BF16),
            jax.ShapeDtypeStruct((2, blocks, count, 128), F32),
            jax.ShapeDtypeStruct((2, blocks, 8, count), F32),
        ),
        grid=(blocks + 1,),
        in_specs=[SMEM]
        + [ANY] * 13
        + [
            pl.BlockSpec((taps, WIDE), lambda i: (0, i)),
            pl.BlockSpec((1, 128), lambda i: (0, 0)),
        ],
        out_specs=(
            pl.BlockSpec((2, count, WIDE), lambda i: (0, 0, head_block(i))),
            pl.BlockSpec((2, count, WIDE), lambda i: (0, 0, head_block(i))),
            pl.BlockSpec((2, 4, ROWS, 128), lambda i: (0, head_block(i), 0, 0)),
            pl.BlockSpec((2, count, STATE), lambda i: (0, 0, 0)),
            pl.BlockSpec((2, count, 256), lambda i: (0, 0, 0)),
            pl.BlockSpec((2, STATE, count), lambda i: (0, 0, 0)),
            pl.BlockSpec((2, blocks, count, 128), lambda i: (0, 0, 0, 0)),
            pl.BlockSpec((2, blocks, 8, count), lambda i: (0, 0, 0, 0)),
        ),
        scratch_shapes=[
            pltpu.VMEM((2 * (count + HALO), width), BF16),
            pltpu.VMEM((2, 8, 4, 4, 32, WIDE), BF16),
            pltpu.VMEM((8, 4, 4, 32, 128), BF16),
            pltpu.VMEM((2 * (count + HALO), WIDE), F32),
            pltpu.VMEM((count + HALO, WIDE), F32),
            pltpu.VMEM((count + HALO, WIDE), F32),
            pltpu.VMEM((2, STATE, count), BF16),
            pltpu.VMEM((2, count, 256), BF16),
            pltpu.VMEM((2, count, 256), BF16),
            pltpu.VMEM((2, 16, 128), BF16),
            pltpu.SemaphoreType.DMA((CHUNKS, 4)),
            pltpu.SemaphoreType.DMA((2, 15)),
        ],
        compiler_params=params(),
        name="mix",
    )(coords, token_rows, other_rows, rims, *pieces, conv, rate)

    def inside(request):
        return pl.pallas_call(
            lambda *refs: inner_kernel(request, *refs),
            out_shape=jax.ShapeDtypeStruct((count, inner), BF16),
            grid=(blocks,),
            in_specs=[
                SMEM,
                pl.BlockSpec((1, count, WIDE), lambda i: (request, 0, i)),
                pl.BlockSpec((1, count, WIDE), lambda i: (request, 0, i)),
                pl.BlockSpec((1, WIDE), lambda i: (0, i)),
                pl.BlockSpec((1, count, STATE), lambda i: (request, 0, 0)),
                pl.BlockSpec((1, STATE, count), lambda i: (request, 0, 0)),
                pl.BlockSpec((1, 1, count, 128), lambda i: (request, i, 0, 0)),
                pl.BlockSpec((1, 1, 8, count), lambda i: (request, i, 0, 0)),
            ],
            out_specs=pl.BlockSpec((count, WIDE), lambda i: (0, i)),
            scratch_shapes=[pltpu.VMEM((count, count), F32)],
            compiler_params=params(),
            cost_estimate=pl.CostEstimate(
                flops=10**10, transcendentals=3 * 10**6, bytes_accessed=6 * 10**6
            ),
            name="inner",
        )(levels, values, driven, skip, query, keys, sums, turned)


    gathered = lax.all_to_all(send.reshape(ring, ROWS, 128), "seq", 0, 0, tiled=True)
    later = inside(1)
    gathered, later = lax.optimization_barrier((gathered, later))
    scanned = pl.pallas_call(
        scan_kernel,
        out_shape=jax.ShapeDtypeStruct((ring, 64, 128), BF16),
        in_specs=[SMEM, SMEM, VMEM],
        out_specs=VMEM,
        scratch_shapes=[pltpu.VMEM((ring, 64, 128), F32), pltpu.VMEM((ring, 64, 128), F32)],
        compiler_params=pltpu.CompilerParams(vmem_limit_bytes=32 * 2**20),
        name="scan",
    )(coords, levels, gathered)
    carried = lax.all_to_all(scanned, "seq", 0, 0, tiled=True)
    carried, sooner = lax.optimization_barrier((carried, inside(0)))
    parts = (sooner, later)

    def finish(request, columns):
        return pl.pallas_call(
            lambda *refs: finish_kernel(request, *refs),
            out_shape=jax.ShapeDtypeStruct((count, columns), BF16),
            grid_spec=pltpu.PrefetchScalarGridSpec(
                num_scalar_prefetch=2,
                grid=(blocks // 2,),
                in_specs=[
                    pl.BlockSpec((count, 2 * WIDE), lambda i, at, facts: (0, i)),
                    pl.BlockSpec((8, 64, 128), lambda i, at, facts: (2 * request + i, 0, 0)),
                    pl.BlockSpec((1, count, STATE), lambda i, at, facts: (request, 0, 0)),
                    pl.BlockSpec((1, count, 256), lambda i, at, facts: (request, 0, 0)),
                ],
                out_specs=pl.BlockSpec(
                    (count, 2 * WIDE),
                    lambda i, at, facts: (0, i if request else at[16] + i),
                ),
            ),
            compiler_params=params(),
            name="finish",
        )(coords, facts, parts[request], carried, query, grow)

    returned = to_twin(finish(1, inner))
    output = finish(0, 2 * inner)
    output = lax.dynamic_update_slice(output, returned, (0, (1 - core) * inner))
    return output.reshape(1, count, 2 * inner)


def solution(mesh):
    in_specs = (P("dp", "seq", None), P(("seq", "dp"), None), P(), P(), P(), P("dp", None), P("dp"))
    out_specs = P("dp", "seq", None)
    return jax.shard_map(body, mesh=mesh, in_specs=in_specs, out_specs=out_specs, check_vma=False)
```

```python
import jax
import jax.numpy as jnp
from jax import lax
from jax.experimental import pallas as pl
from jax.experimental.pallas import tpu as pltpu
from jax.sharding import PartitionSpec as P


STATE = 128
HALO = 16
WIDE = 256
ROWS = 72
UNIT = 16
SHARE = 11 * UNIT
CHUNKS = 8
SEGMENTS = (
    ((0, 0, 32, 0),),
    ((0, 32, 32, 0),),
    ((0, 64, 32, 0),),
    ((0, 96, 32, 0),),
    ((0, 128, 32, 0),),
    ((0, 160, 16, 0), (1, 0, 16, 16)),
) + tuple(((1, 16 + 32 * i, 32, 0),) for i in range(5))
F32 = jnp.float32
BF16 = jnp.bfloat16


def dot(a, b):
    return jnp.dot(a, b, preferred_element_type=F32)


def two_parts(x):
    high = x.astype(BF16)
    return high, (x - high.astype(F32)).astype(BF16)


def spread(block, width):
    head = lax.broadcasted_iota(jnp.int32, (2 * 128, width), 0) & 127
    lane = lax.broadcasted_iota(jnp.int32, (2 * 128, width), 1)
    return jnp.where(head == 4 * block + (lane >> 6), 1.0, 0.0).astype(BF16)


def split_three(x):
    first = x.astype(BF16)
    rest = x - first.astype(F32)
    second = rest.astype(BF16)
    return first, second, (rest - second.astype(F32)).astype(BF16)


def mix_kernel(
    coord_ref, own_ref, other_ref, rims_ref,
    a0, a1, a2, a3, a4, b0, b1, b2, b3, b4,
    conv_ref, rate_ref,
    values_ref, driven_ref, send_ref, query_ref, grow_ref, keys_ref, sums_s, sums_t,
    tok_s, w_s, small_s, proj_s, raw_a, raw_b, spread_s, keys_s, step_s, fade_s, total_s,
    tok_sem, w_sem,
):
    count = own_ref.shape[0]
    pitch = count + HALO
    width = own_ref.shape[1]
    chunk = width // CHUNKS
    step = pl.program_id(0)
    steps = 5
    block = step - 1

    def weight_copies(at):
        slot = at % 2
        columns = (0, 1, 2) if at == 0 else (2 * at + 1, 2 * at + 2)
        copies = []
        for index, column in enumerate(columns):
            if column == 2:
                target, lanes = small_s, slice(0, 128)
            else:
                target, lanes = w_s.at[slot], slice(index * 128, index * 128 + 128)
            for part, row, rows, offset in SEGMENTS[column]:
                into = slice(offset, offset + rows)
                for piece, ref in enumerate(((a0, a1, a2, a3, a4), (b0, b1, b2, b3, b4))[part]):
                    planes = (slice(0, 8), slice(0, 8), slice(0, 8), slice(0, 4), slice(4, 8))[piece]
                    where = coord_ref[4 * part + min(piece, 3)]
                    source = ref.at[:, :, row : row + rows, :]
                    if part == 0:
                        sink = target.at[planes, :, where, into, lanes]
                    else:
                        sink = target.at[planes, where, :, into, lanes]
                    copies.append(pltpu.make_async_copy(source, sink, w_sem.at[slot, len(copies)]))
        return copies

    def token_copies(at):
        lanes = slice(at * chunk, at * chunk + chunk)
        pairs = (
            (rims_ref.at[0:HALO, lanes], tok_s.at[0:HALO, lanes]),
            (own_ref.at[:, lanes], tok_s.at[HALO:pitch, lanes]),
            (rims_ref.at[HALO : 2 * HALO, lanes], tok_s.at[pitch : pitch + HALO, lanes]),
            (other_ref.at[:, lanes], tok_s.at[pitch + HALO : 2 * pitch, lanes]),
        )
        return [
            pltpu.make_async_copy(source, sink, tok_sem.at[at, place])
            for place, (source, sink) in enumerate(pairs)
        ]

    @pl.when(step == 0)
    def _():
        for copy in weight_copies(0):
            copy.start()
        for at in range(CHUNKS):
            for copy in token_copies(at):
                copy.start()
        for copy in weight_copies(1):
            copy.start()
        for copy in weight_copies(0):
            copy.wait()

    def project(request, slot):
        rows = tok_s[request * pitch : request * pitch + pitch]
        return dot(rows, w_s[slot].reshape(width, WIDE))

    def convolve(raw):
        taps = conv_ref.shape[0]
        total = None
        for tap in range(taps):
            late = taps - 1 - tap
            moved = raw if late == 0 else pltpu.roll(raw, late, 0)
            part = moved[HALO:] * conv_ref[tap : tap + 1, :]
            total = part if total is None else total + part
        return total

    @pl.when(step == 0)
    def _():
        planes = 8 // CHUNKS
        for at in range(CHUNKS):
            for copy in token_copies(at):
                copy.wait()
            token = tok_s[:, at * chunk : at * chunk + chunk]
            main = dot(token, w_s[0, at * planes : (at + 1) * planes].reshape(chunk, WIDE))
            small = dot(token, small_s[at * planes : (at + 1) * planes].reshape(chunk, 128))
            if at == 0:
                proj_s[...] = main
                raw_b[:, :128] = small[:pitch]
                raw_b[:, 128:] = small[pitch:]
            else:
                proj_s[...] += main
                raw_b[:, :128] += small[:pitch]
                raw_b[:, 128:] += small[pitch:]
        for copy in weight_copies(2):
            copy.start()
        for copy in weight_copies(1):
            copy.wait()
        raw_a[...] = project(0, 1)
        row = lax.broadcasted_iota(jnp.int32, (count, count), 0)
        col = lax.broadcasted_iota(jnp.int32, (count, count), 1)
        lower = jnp.where(col <= row, 1.0, 0.0).astype(BF16)
        for request in range(2):
            x = raw_b[pl.ds(HALO, count), 128 * request : 128 * request + 128]
            size = jnp.maximum(x, 0.0) + jnp.log1p(jnp.exp(-jnp.abs(x)))
            first, second, third = split_three(-size * rate_ref[...])
            sums = dot(lower, first) + dot(lower, second) + dot(lower, third)
            turned = sums.T
            for group in range(4):
                sums_t[request, group] = turned[4 * group : 4 * group + 8]
                sums_s[request, group] = sums if group == 0 else pltpu.roll(sums, 128 - 4 * group, 1)
            step_s[request, :, :128], step_s[request, :, 128:] = two_parts(size)
            fade = jnp.exp(sums[count - 1 :] - sums)
            fade_s[request, :, :128], fade_s[request, :, 128:] = two_parts(fade)
            grow_ref[request, :, :128], grow_ref[request, :, 128:] = two_parts(jnp.exp(sums))
            first, second, third = split_three(jnp.broadcast_to(sums[count - 1 :], (16, 128)))
            place = lax.broadcasted_iota(jnp.int32, (16, 128), 0)
            total = jnp.where(
                place == 0,
                first.astype(F32),
                jnp.where(
                    place == 1, second.astype(F32), jnp.where(place == 2, third.astype(F32), 0.0)
                ),
            )
            total_s[request] = total.astype(BF16)
        for request in range(2):
            mixed = convolve(proj_s[request * pitch : request * pitch + pitch]).astype(BF16)
            query = mixed[:, STATE:]
            query_ref[request] = query
            keys_t = mixed[:, :STATE].astype(F32).T.astype(BF16)
            keys_s[request] = keys_t
            keys_ref[request] = keys_t

    def drive(request, source, lanes):
        convolved = convolve(source[...])
        half = 0.5 * convolved
        values = (half + half * jnp.tanh(half)).astype(BF16)
        values_ref[request] = values
        driven = (values.astype(F32) * dot(step_s[request], lanes)).astype(BF16)
        driven_ref[request] = driven
        faded = (driven.astype(F32) * dot(fade_s[request], lanes)).astype(BF16)
        states = dot(keys_s[request], faded).astype(BF16)
        totals = dot(total_s[request], lanes[:128]).astype(BF16)
        for unit in range(4):
            pair, half = unit // 2, unit % 2
            cut = slice(pair * 128, pair * 128 + 128)
            send_ref[request, unit, :64] = states[half * 64 : half * 64 + 64, cut]
            send_ref[request, unit, 64:] = totals[: ROWS - 64, cut]

    @pl.when(step >= 1)
    def _():
        raw_b[...] = project(1, step % 2)
        lanes = spread(block, WIDE)
        spread_s[...] = lanes
        drive(0, raw_a, lanes)

    for at in range(1, steps - 1):

        @pl.when(step == at)
        def _(at=at):
            if at + 2 < steps:
                for copy in weight_copies(at + 2):
                    copy.start()
            for copy in weight_copies(at + 1):
                copy.wait()

    @pl.when(step >= 1)
    def _():
        raw_a[...] = project(0, (step + 1) % 2)
        drive(1, raw_b, spread_s[...])


def inner_kernel(
    request, level_ref, values_ref, driven_ref, skip_ref, query_ref, keys_ref, sums_ref, turned_ref,
    part_ref, score_s,
):
    count = part_ref.shape[0]

    @pl.when(pl.program_id(0) == 0)
    def _():
        row = lax.broadcasted_iota(jnp.int32, (count, count), 0)
        col = lax.broadcasted_iota(jnp.int32, (count, count), 1)
        apart = (row >> 6) ^ (col >> 6)
        weight = jnp.where(
            apart == 0,
            level_ref[request, 0],
            jnp.where(
                apart == 1,
                level_ref[request, 1],
                jnp.where(apart < 4, level_ref[request, 2], level_ref[request, 3]),
            ),
        )
        score_s[...] = dot(query_ref[0], keys_ref[0]) * jnp.where(col <= row, weight, 0.0)

    side = lax.broadcasted_iota(jnp.int32, (count, 128), 1) < 64
    for pair in range(2):
        cut = slice(pair * 128, pair * 128 + 128)
        both = driven_ref[0, :, cut]
        sides = (
            jnp.where(side, both, jnp.zeros_like(both)),
            jnp.where(side, jnp.zeros_like(both), both),
        )
        for tile in range(count // 128):
            top, reach = tile * 128, tile * 128 + 128
            total = values_ref[0, top:reach, cut].astype(F32) * skip_ref[:, cut]
            score = score_s[top:reach, :reach]
            for half in range(2):
                head = 2 * pair + half
                later = sums_ref[0, 0, top:reach, head : head + 1]
                earlier = turned_ref[0, 0, head : head + 1, :reach]
                weight = score * jnp.exp(jnp.minimum(later - earlier, 0.0))
                total = total + dot(weight.astype(BF16), sides[half][:reach])
            part_ref[top:reach, cut] = total.astype(BF16)


def order_z_kernel(coord_ref, *refs):
    pieces, outs = refs[:8], refs[8:]
    for part in range(2):
        for place in range(8):
            outs[part][coord_ref[8 + place]] = pieces[place][part]


def order_kernel(base, coord_ref, *refs):
    pieces, out_ref = refs[:4], refs[4]
    for place in range(4):
        out_ref[:, coord_ref[base + place]] = pieces[place][...]


def scan_kernel(coord_ref, level_ref, state_ref, out_ref, sum_s, block_s):
    count = state_ref.shape[0]
    request = coord_ref[17]
    totals = []
    for place in range(count):
        rows = state_ref[place, 64:ROWS].astype(F32)
        totals.append(rows[0:1] + rows[1:2] + rows[2:3])
    before = [jnp.zeros_like(totals[0])]
    for place in range(count - 1):
        before.append(before[-1] + totals[place])
    sum_s[...] = jnp.zeros_like(sum_s)
    for place in range(count):
        block_s[place] = state_ref[place, :64].astype(F32)
    level = 0
    while (1 << level) < count:
        span = 1 << level
        for start in range(span, count, 2 * span):
            previous = block_s[start - span] * level_ref[request, 4 + level]
            for place in range(start, start + span):
                sum_s[place] += jnp.exp(before[place] - before[start]) * previous
            end = start + span
            gone = totals[start]
            for place in range(start + 1, end):
                gone = gone + totals[place]
            block_s[start - span] = block_s[start - span] * jnp.exp(gone) + block_s[start]
        level += 1
    out_ref[...] = sum_s[...].astype(BF16)


def finish_kernel(request, coord_ref, fact_ref, part_ref, state_ref, query_ref, grow_ref, out_ref):
    count = part_ref.shape[0]
    block = pl.program_id(0)
    grow = dot(grow_ref[0], spread(2 * block, 2 * WIDE))
    first = lax.broadcasted_iota(jnp.int32, (128, 128), 0)
    second = lax.broadcasted_iota(jnp.int32, (128, 128), 1)
    ones = jnp.where((first >> 6) == (second >> 6), 1.0, 0.0).astype(BF16)
    spot = coord_ref[18] + lax.broadcasted_iota(jnp.int32, (count, 128), 0)
    live = spot < fact_ref[request, 11]
    for pair in range(4):
        lanes = slice(pair * 128, pair * 128 + 128)
        state = jnp.concatenate([state_ref[2 * pair], state_ref[2 * pair + 1]], 0)
        y = part_ref[:, lanes].astype(F32) + grow[:, lanes] * dot(query_ref[0], state)
        mean = dot((y * y).astype(BF16), ones) * (1.0 / 64.0)
        y = y * lax.rsqrt(mean + 1e-05)
        out_ref[:, lanes] = jnp.where(live, y, 0.0).astype(BF16)


def params():
    return pltpu.CompilerParams(dimension_semantics=("arbitrary",), vmem_limit_bytes=56 * 2**20)


ANY = pl.BlockSpec(memory_space=pl.ANY)
VMEM = pl.BlockSpec(memory_space=pltpu.VMEM)
SMEM = pl.BlockSpec(memory_space=pltpu.SMEM)


def near(i):
    return i ^ 1


def far(i):
    return ((i + 1) ^ 1) - 1


def along(value, axis, kind):
    pairs = []
    for i in range(256):
        place = {"z": i // 32, "x": i // 8 % 4, "y": i // 2 % 4}
        core = i % 2
        size = 8 if axis == "z" else 4
        move = near if core == kind else far
        place[axis] = move(place[axis]) % size
        pairs.append((i, ((place["z"] * 4 + place["x"]) * 4 + place["y"]) * 2 + core))
    return lax.ppermute(value, ("seq", "dp"), pairs)


def to_twin(value):
    return lax.ppermute(value, "dp", [(i, i ^ 1) for i in range(8)])


def ring_of_four(value, axis):
    first = along(value, axis, 0)
    second = along(value, axis, 1)
    return (value, first, second, along(second, axis, 0))


def halved_ring(value, axis, extra=None):
    half = value.shape[0] // 2
    first = along(value, axis, 0)
    second = along(value, axis, 1)
    if extra is not None:
        second, extra = lax.optimization_barrier((second, extra))
    return extra, (
        value, first, second, along(second[:half], axis, 0), along(first[half:], axis, 1)
    )


def ordered(pieces, coords, base, name):
    shape = pieces[0].shape
    return pl.pallas_call(
        lambda *refs: order_kernel(base, *refs),
        out_shape=jax.ShapeDtypeStruct((shape[0], 4) + shape[1:], BF16),
        in_specs=[SMEM] + [VMEM] * 4,
        out_specs=VMEM,
        name=name,
    )(coords, *pieces)


def gather_weights(w_in, core, coords, extra):
    depth = w_in.shape[0]
    tiles = w_in[:, :2304].reshape(depth, 18, 128).transpose(1, 0, 2)

    def share(of):
        small = lax.dynamic_slice(w_in, (0, 2304 + 16 * of), (depth, 16))
        small = jnp.pad(small, ((0, 0), (0, 112)))[None]
        return jnp.concatenate([tiles[16:], small, lax.dynamic_slice_in_dim(tiles, 8 * of, 8)], 0)

    mine = share(core)
    got = to_twin(share(1 - core))
    low = jnp.where(core == 0, mine, got)
    high = jnp.where(core == 0, got, mine)
    start = jnp.stack([low, high], 1).reshape(2, SHARE, 128)
    a1, b1 = along(start, "z", 0), along(start, "z", 1)
    a2, b2 = along(b1, "z", 0), along(a1, "z", 1)
    a3, b3 = along(b2, "z", 0), along(a2, "z", 1)
    a4 = along(b3, "z", 0)
    first, second = pl.pallas_call(
        order_z_kernel,
        out_shape=(jax.ShapeDtypeStruct((8, SHARE, 128), BF16),) * 2,
        in_specs=[SMEM] + [VMEM] * 8,
        out_specs=(VMEM, VMEM),
        name="order_z",
    )(coords, start, a1, b1, a2, b2, a3, b3, a4)
    first = ordered(ring_of_four(first, "x"), coords, 4, "order_x")
    second = ordered(ring_of_four(second, "y"), coords, 0, "order_y")
    rest, back = halved_ring(second, "x", extra(got))
    _, front = halved_ring(first, "y")
    return rest, front + back


def body(tokens, w_in, conv_w, a_rate, d_skip, level_w, lengths):
    token_rows = tokens.reshape(-1, tokens.shape[-1])
    count, width = token_rows.shape
    taps, channels = conv_w.shape
    heads = a_rate.shape[0] // 2
    inner = (channels - 2 * STATE) // 2
    head_dim = inner // heads
    blocks = inner // WIDE
    ring = lax.axis_size("seq")
    position = lax.axis_index("seq")
    line = lax.axis_index("dp")
    core = line % 2
    y, x, z = line // 2, position % 4, position // 4

    def one(i, size):
        return jnp.where(core == 0, i ^ 1, jnp.mod(((i + 1) ^ 1) - 1, size))

    def two(i, size):
        return jnp.where(core == 0, jnp.mod(((i + 1) ^ 1) - 1, size), i ^ 1)

    trail = [z, one(z, 8), two(z, 8)]
    trail += [two(trail[1], 8), one(trail[2], 8)]
    trail += [one(trail[3], 8), two(trail[4], 8), jnp.mod(z + 4, 8)]
    coords = jnp.stack(
        [y, one(y, 4), two(y, 4), y ^ 2, x, one(x, 4), two(x, 4), x ^ 2]
        + trail
        + [core * blocks // 2, position // 16, position * count]
    )
    coords = coords.astype(jnp.int32)

    def extra(got):
        rows, _ = lax.optimization_barrier((token_rows, got))
        other_rows = to_twin(rows)
        tails = jnp.stack([token_rows[count - taps + 1 :], other_rows[count - taps + 1 :]])
        rims = lax.ppermute(tails, "seq", [(i, i + 1) for i in range(ring - 1)])
        rims = jnp.pad(rims, ((0, 0), (HALO - taps + 1, 0), (0, 0))).reshape(2 * HALO, width)
        facts = jnp.concatenate([level_w.reshape(-1), lengths, jnp.zeros((4,), jnp.int32)])
        facts = jnp.stack([facts, to_twin(facts)])
        levels = facts.astype(F32) / 256.0
        rate = jnp.pad(lax.dynamic_slice(a_rate, (core * heads,), (heads,)), (0, 128 - heads))
        skip = jnp.repeat(lax.dynamic_slice(d_skip, (core * heads,), (heads,)), head_dim)
        own_conv = lax.dynamic_slice(conv_w, (0, core * inner), (taps, inner))
        conv = jnp.concatenate([conv_w[:, 2 * inner :], own_conv], 1)
        return rims, other_rows, facts, levels, rate[None], skip[None], conv

    rest, pieces = gather_weights(w_in, core, coords, extra)
    rims, other_rows, facts, levels, rate, skip, conv = rest

    def head_block(i):
        return jnp.maximum(i - 1, 0)

    values, driven, send, query, grow, keys, sums, turned = pl.pallas_call(
        mix_kernel,
        out_shape=(
            jax.ShapeDtypeStruct((2, count, inner), BF16),
            jax.ShapeDtypeStruct((2, count, inner), BF16),
            jax.ShapeDtypeStruct((2, heads, ROWS, 128), BF16),
            jax.ShapeDtypeStruct((2, count, STATE), BF16),
            jax.ShapeDtypeStruct((2, count, 256), BF16),
            jax.ShapeDtypeStruct((2, STATE, count), BF16),
            jax.ShapeDtypeStruct((2, blocks, count, 128), F32),
            jax.ShapeDtypeStruct((2, blocks, 8, count), F32),
        ),
        grid=(blocks + 1,),
        in_specs=[SMEM]
        + [ANY] * 13
        + [
            pl.BlockSpec((taps, WIDE), lambda i: (0, i)),
            pl.BlockSpec((1, 128), lambda i: (0, 0)),
        ],
        out_specs=(
            pl.BlockSpec((2, count, WIDE), lambda i: (0, 0, head_block(i))),
            pl.BlockSpec((2, count, WIDE), lambda i: (0, 0, head_block(i))),
            pl.BlockSpec((2, 4, ROWS, 128), lambda i: (0, head_block(i), 0, 0)),
            pl.BlockSpec((2, count, STATE), lambda i: (0, 0, 0)),
            pl.BlockSpec((2, count, 256), lambda i: (0, 0, 0)),
            pl.BlockSpec((2, STATE, count), lambda i: (0, 0, 0)),
            pl.BlockSpec((2, blocks, count, 128), lambda i: (0, 0, 0, 0)),
            pl.BlockSpec((2, blocks, 8, count), lambda i: (0, 0, 0, 0)),
        ),
        scratch_shapes=[
            pltpu.VMEM((2 * (count + HALO), width), BF16),
            pltpu.VMEM((2, 8, 4, 4, 32, WIDE), BF16),
            pltpu.VMEM((8, 4, 4, 32, 128), BF16),
            pltpu.VMEM((2 * (count + HALO), WIDE), F32),
            pltpu.VMEM((count + HALO, WIDE), F32),
            pltpu.VMEM((count + HALO, WIDE), F32),
            pltpu.VMEM((256, WIDE), BF16),
            pltpu.VMEM((2, STATE, count), BF16),
            pltpu.VMEM((2, count, 256), BF16),
            pltpu.VMEM((2, count, 256), BF16),
            pltpu.VMEM((2, 16, 128), BF16),
            pltpu.SemaphoreType.DMA((CHUNKS, 4)),
            pltpu.SemaphoreType.DMA((2, 15)),
        ],
        compiler_params=params(),
        name="mix",
    )(coords, token_rows, other_rows, rims, *pieces, conv, rate)

    def inside(request):
        return pl.pallas_call(
            lambda *refs: inner_kernel(request, *refs),
            out_shape=jax.ShapeDtypeStruct((count, inner), BF16),
            grid=(blocks,),
            in_specs=[
                SMEM,
                pl.BlockSpec((1, count, WIDE), lambda i: (request, 0, i)),
                pl.BlockSpec((1, count, WIDE), lambda i: (request, 0, i)),
                pl.BlockSpec((1, WIDE), lambda i: (0, i)),
                pl.BlockSpec((1, count, STATE), lambda i: (request, 0, 0)),
                pl.BlockSpec((1, STATE, count), lambda i: (request, 0, 0)),
                pl.BlockSpec((1, 1, count, 128), lambda i: (request, i, 0, 0)),
                pl.BlockSpec((1, 1, 8, count), lambda i: (request, i, 0, 0)),
            ],
            out_specs=pl.BlockSpec((count, WIDE), lambda i: (0, i)),
            scratch_shapes=[pltpu.VMEM((count, count), F32)],
            compiler_params=params(),
            cost_estimate=pl.CostEstimate(
                flops=10**10, transcendentals=3 * 10**6, bytes_accessed=6 * 10**6
            ),
            name="inner",
        )(levels, values, driven, skip, query, keys, sums, turned)


    gathered = lax.all_to_all(send.reshape(ring, ROWS, 128), "seq", 0, 0, tiled=True)
    later = inside(1)
    gathered, later = lax.optimization_barrier((gathered, later))
    scanned = pl.pallas_call(
        scan_kernel,
        out_shape=jax.ShapeDtypeStruct((ring, 64, 128), BF16),
        in_specs=[SMEM, SMEM, VMEM],
        out_specs=VMEM,
        scratch_shapes=[pltpu.VMEM((ring, 64, 128), F32), pltpu.VMEM((ring, 64, 128), F32)],
        compiler_params=pltpu.CompilerParams(vmem_limit_bytes=32 * 2**20),
        name="scan",
    )(coords, levels, gathered)
    carried = lax.all_to_all(scanned, "seq", 0, 0, tiled=True)
    carried, sooner = lax.optimization_barrier((carried, inside(0)))
    parts = (sooner, later)

    def finish(request, columns):
        return pl.pallas_call(
            lambda *refs: finish_kernel(request, *refs),
            out_shape=jax.ShapeDtypeStruct((count, columns), BF16),
            grid_spec=pltpu.PrefetchScalarGridSpec(
                num_scalar_prefetch=2,
                grid=(blocks // 2,),
                in_specs=[
                    pl.BlockSpec((count, 2 * WIDE), lambda i, at, facts: (0, i)),
                    pl.BlockSpec((8, 64, 128), lambda i, at, facts: (2 * request + i, 0, 0)),
                    pl.BlockSpec((1, count, STATE), lambda i, at, facts: (request, 0, 0)),
                    pl.BlockSpec((1, count, 256), lambda i, at, facts: (request, 0, 0)),
                ],
                out_specs=pl.BlockSpec(
                    (count, 2 * WIDE),
                    lambda i, at, facts: (0, i if request else at[16] + i),
                ),
            ),
            compiler_params=params(),
            name="finish",
        )(coords, facts, parts[request], carried, query, grow)

    returned = to_twin(finish(1, inner))
    output = finish(0, 2 * inner)
    output = lax.dynamic_update_slice(output, returned, (0, (1 - core) * inner))
    return output.reshape(1, count, 2 * inner)


def solution(mesh):
    in_specs = (P("dp", "seq", None), P(("seq", "dp"), None), P(), P(), P(), P("dp", None), P("dp"))
    out_specs = P("dp", "seq", None)
    return jax.shard_map(body, mesh=mesh, in_specs=in_specs, out_specs=out_specs, check_vma=False)
```
